128 devices in a mesh: tm: 8 (over z_hi, x), space: 16 (over z_lo, y, core).
Axes of the slice: x: 4, y: 4, z: 4 (z_hi: 2, z_lo: 2; z = z_hi * 2 + z_lo), core: 2. Of those that a mesh axis runs over, the one named last changes fastest.
Arguments:
- snapshots: float32 [256, 3, 16, 32, 128], P('tm', None, 'space'), may hold values from -6 to 6
- coeffs: float32 [256, 128], replicated, may hold values from -0.375 to 0.375
- pair_table: int32 [4096, 2], replicated, may hold values from 0 to 127
Outputs:
- tensor: float32 [4096, 128], P(('tm', 'space'))
The draws below stay inside these ranges and needn't reach their ends.
Inputs may be any that keep to these rules, and one draw needn't show every extreme that they name: `pair_table`: column 0 names the carrying mode, column 1 the carried mode.
All inputs are finite; a program needn't handle non-finite values.
Results may differ from the reference program's by a relative error of at most 0.00016.
Values sent between devices are 32-bit elements; how exact they have to be, the bound alone decides.
A program may use at most 192 MiB of HBM per device.

```python
import math
import jax
import jax.numpy as jnp
from jax import lax

M = 128
NZ = 128
S = 256
NX = 16
NY = 32
PAIRS = 4096


def touch_ends(values, stream_key, least, high):
    place = [jax.random.randint(jax.random.fold_in(stream_key, axis), (), 0, length) for axis, length in enumerate(values.shape)]
    longest = values.shape.index(max(values.shape))
    neighbour = place[:longest] + [(place[longest] + 1) % values.shape[longest]] + place[longest + 1:]
    return values.at[tuple(place)].set(least).at[tuple(neighbour)].set(high)


def level_of(stream_key, shape, cuts, low, high):
    gain, own = 1.0, jax.random.fold_in(stream_key, 6)
    for position, shards_of in cuts:
        draws = jnp.exp(jax.random.uniform(jax.random.fold_in(own, position), (shards_of,), jnp.float32, low / len(cuts), high / len(cuts)))
        gain = gain * jnp.repeat(draws, shape[position] // shards_of).reshape([-1 if axis == position else 1 for axis in range(len(shape))])
    return gain


def noise(stream_key, dims, spread, reach, cuts=(), held_as=jnp.bfloat16):
    factor_of = level_of(stream_key, dims, cuts, -0.22, 0.18) if cuts else 1.0
    array = jax.random.normal(stream_key, dims, jnp.float32) * spread * factor_of
    return jnp.minimum(jnp.maximum(array, -reach), reach).astype(held_as)


def setup_inputs(seed: int = 0) -> dict:
    splits = jax.random.split(jax.random.key(seed), 4)
    snapshots = noise(splits[0], (S, 3, NX, NY, NZ), 1.0, 6.0, ((0, 8), (2, 16)), jnp.float32)
    coeffs = noise(splits[1], (S, M), S ** -0.5, 0.375, (), jnp.float32)
    pair_table = touch_ends(jax.random.randint(splits[2], (PAIRS, 2), 0, M), jax.random.fold_in(splits[2], 1), 0, M - 1).astype(jnp.int32)
    return {"snapshots": snapshots, "coeffs": coeffs, "pair_table": pair_table}


def gradient_field(mode_field):
    padded_y = jnp.pad(mode_field, ((0, 0), (0, 0), (0, 0), (1, 1), (0, 0)))
    stream_slope = (jnp.roll(mode_field, -1, 2) - jnp.roll(mode_field, 1, 2)) * 0.5
    normal_slope = (padded_y[:, :, :, 2:] - padded_y[:, :, :, :-2]) * 0.5
    span_slope = (jnp.roll(mode_field, -1, 4) - jnp.roll(mode_field, 1, 4)) * 0.5
    return jnp.stack([stream_slope, normal_slope, span_slope], axis=1)


def pair_block(pair_rows, flat_modes, flat_slopes):
    first_modes = jnp.take(flat_modes, pair_rows[:, 0], axis=0)
    second_slopes = jnp.take(flat_slopes, pair_rows[:, 1], axis=0)
    convection = jnp.einsum('bdl,bdcl->bcl', first_modes, second_slopes, precision=lax.Precision.HIGHEST)
    return jnp.einsum('bcl,kcl->bk', convection, flat_modes, precision=lax.Precision.HIGHEST)


def reference(snapshots, coeffs, pair_table):
    mode_field = jnp.einsum('sk,scxyz->kcxyz', coeffs, snapshots, precision=lax.Precision.HIGHEST)
    slopes = gradient_field(mode_field)
    flat_modes = mode_field.reshape(M, 3, -1)
    flat_slopes = slopes.reshape(M, 3, 3, -1)
    group_size = math.gcd(PAIRS, 64)
    grouped = pair_table.reshape(PAIRS // group_size, group_size, 2)

    def one_group(group_rows):
        return pair_block(group_rows, flat_modes, flat_slopes)

    result = lax.map(one_group, grouped)
    return result.reshape(PAIRS, M) * (float(NX * NY * NZ) ** -0.5)
```

```python
import functools

import jax
import jax.numpy as jnp
from jax import lax
from jax.experimental import pallas as pl
from jax.experimental.pallas import tpu as pltpu
from jax.sharding import PartitionSpec as P

MESH = pl.DeviceIdType.MESH
F32 = jnp.float32
BF16 = jnp.bfloat16
MODES = 128
LANES = 128
PAIRS = 4096
STEP = 48
BLOCK = 512


def here():
    t, s = lax.axis_index("tm"), lax.axis_index("space")
    return lax.rem(t, 4), lax.rem(lax.div(s, 2), 4), lax.div(t, 4), lax.div(s, 8), lax.rem(s, 2)


def there(x, y, zh, zl, core):
    return zh * 4 + x, zl * 8 + y * 2 + core


def band_of(x, zh):
    return x + zh * (7 - 2 * x)


def owner_of(band):
    zh = lax.div(band, 4)
    return zh * 4 + band + zh * (7 - 2 * band)


def split(value):
    high = value.astype(BF16)
    return high, (value - high.astype(F32)).astype(BF16)


def dot(a, b):
    return jnp.dot(a, b, preferred_element_type=F32)


ORDER = (5, 2, 7, 4, 1, 6, 3)


def tables_kernel(
    snaps, coeffs, u_tab, s_tab, rhs, send, recv, modes, below, above, low, high,
    own_sem, a2a_s, a2a_r, x_s, x_r, y_s, y_r,
):
    x, y, zh, zl, core = here()
    tm, space = lax.axis_index("tm"), lax.axis_index("space")
    band = band_of(x, zh)
    after, before = lax.rem(space + 1, 16), lax.rem(space + 15, 16)

    def partner(rel):
        return lax.rem(zh + rel // 4, 2) * 4 + lax.rem(x + rel % 4, 4)

    barrier = pltpu.get_barrier_semaphore()
    for rel in range(1, 8):
        pl.semaphore_signal(barrier, inc=1, device_id=(partner(rel), space), device_id_type=MESH)
    for side in (after, before):
        pl.semaphore_signal(barrier, inc=1, device_id=(tm, side), device_id_type=MESH)

    for b in range(8):
        for c in range(3):
            for r in range(4):
                send[b, c * 4 + r] = snaps[pl.ds(c * 32 + 4 * b + r, 32, stride=96), :]
    own = pltpu.make_async_copy(send.at[band], recv.at[:, pl.ds(tm * 32, 32), :], own_sem)
    own.start()
    pl.semaphore_wait(barrier, 9)

    def exchange(c, rel):
        t = partner(rel)
        zt, xt = lax.div(t, 4), lax.rem(t, 4)
        return pltpu.make_async_remote_copy(
            src_ref=send.at[band_of(xt, zt), pl.ds(c * 4, 4)],
            dst_ref=recv.at[pl.ds(c * 4, 4), pl.ds(tm * 32, 32), :],
            send_sem=a2a_s.at[c, rel], recv_sem=a2a_r.at[c, rel],
            device_id=(t, space), device_id_type=MESH,
        )

    def x_copy(c, up):
        return pltpu.make_async_remote_copy(
            src_ref=modes.at[pl.ds(c * 4, 4)],
            dst_ref=(below if up else above).at[pl.ds(c * 4, 4)],
            send_sem=x_s.at[c, up], recv_sem=x_r.at[c, up],
            device_id=(tm, after if up else before), device_id_type=MESH,
        )

    def y_copy(c, up):
        target = owner_of(jnp.minimum(band + 1, 7) if up else jnp.maximum(band - 1, 0))
        return pltpu.make_async_remote_copy(
            src_ref=modes.at[c * 4 + (3 if up else 0)],
            dst_ref=(low if up else high).at[c],
            send_sem=y_s.at[c, up], recv_sem=y_r.at[c, up],
            device_id=(target, space), device_id_type=MESH,
        )

    for c in range(3):
        for rel in ORDER:
            exchange(c, rel).start()

    @pl.when(band == 0)
    def _():
        low[...] = jnp.zeros_like(low)

    @pl.when(band == 7)
    def _():
        high[...] = jnp.zeros_like(high)

    coeff_high, coeff_low = split(coeffs[...].T)
    own.wait()
    for c in range(3):
        for rel in ORDER:
            exchange(c, rel).wait_recv()
        rows = jnp.concatenate([recv[c * 4 + r] for r in range(4)], axis=1)
        row_high, row_low = split(rows)
        field = dot(coeff_high, row_high) + dot(coeff_high, row_low) + dot(coeff_low, row_high)
        for r in range(4):
            modes[c * 4 + r] = field[:, r * 128 : r * 128 + 128]
        for up in (1, 0):
            x_copy(c, up).start()

        @pl.when(band < 7)
        def _():
            y_copy(c, 1).start()

        @pl.when(band > 0)
        def _():
            y_copy(c, 0).start()

        for r in range(4):
            half, row = r // 2, r % 2
            value = field[:, r * 128 : r * 128 + 128]
            slot = half * 24 + c * 8 + row
            for copy in range(3):
                u_tab[pl.ds(slot + 2 * copy, MODES, stride=STEP), :] = value
            turned_high, turned_low = split(value.T)
            at = (half * 6 + c * 2 + row) * LANES
            rhs[at : at + LANES, 0:128] = turned_high
            rhs[at : at + LANES, 128:256] = turned_low
            slope = pltpu.roll(value, 127, 1) - pltpu.roll(value, 1, 1)
            s_tab[pl.ds(half * 24 + 16 + c * 2 + row, MODES, stride=STEP), :] = slope

    for c in range(3):
        @pl.when(band > 0)
        def _():
            y_copy(c, 1).wait_recv()

        @pl.when(band < 7)
        def _():
            y_copy(c, 0).wait_recv()

        for r in range(4):
            half, row = r // 2, r % 2
            under = low[c] if r == 0 else modes[c * 4 + r - 1]
            over = high[c] if r == 3 else modes[c * 4 + r + 1]
            s_tab[pl.ds(half * 24 + 8 + c * 2 + row, MODES, stride=STEP), :] = over - under
        for up in (1, 0):
            x_copy(c, up).wait_recv()
        for r in range(4):
            half, row = r // 2, r % 2
            slope = above[c * 4 + r] - below[c * 4 + r]
            s_tab[pl.ds(half * 24 + c * 2 + row, MODES, stride=STEP), :] = slope

    for c in range(3):
        for rel in ORDER:
            exchange(c, rel).wait_send()
        for up in (1, 0):
            x_copy(c, up).wait_send()

        @pl.when(band < 7)
        def _():
            y_copy(c, 1).wait_send()

        @pl.when(band > 0)
        def _():
            y_copy(c, 0).wait_send()


def make_tables(snaps, coeffs):
    vmem = pl.BlockSpec(memory_space=pltpu.VMEM)
    dma = pltpu.SemaphoreType.DMA
    return pl.pallas_call(
        tables_kernel,
        out_shape=[
            jax.ShapeDtypeStruct((MODES * STEP, LANES), F32),
            jax.ShapeDtypeStruct((MODES * STEP, LANES), F32),
            jax.ShapeDtypeStruct((12 * LANES, 256), BF16),
        ],
        in_specs=[vmem, vmem],
        out_specs=[vmem, vmem, vmem],
        scratch_shapes=[
            pltpu.VMEM((8, 12, 32, LANES), F32),
            pltpu.VMEM((12, 256, LANES), F32),
            pltpu.VMEM((12, MODES, LANES), F32),
            pltpu.VMEM((12, MODES, LANES), F32),
            pltpu.VMEM((12, MODES, LANES), F32),
            pltpu.VMEM((3, MODES, LANES), F32),
            pltpu.VMEM((3, MODES, LANES), F32),
            dma, dma((3, 8)), dma((3, 8)), dma((3, 2)), dma((3, 2)), dma((3, 2)), dma((3, 2)),
        ],
        compiler_params=pltpu.CompilerParams(
            collective_id=0, has_side_effects=True, vmem_limit_bytes=48 * 2**20
        ),
        name="tables",
    )(snaps, coeffs)


def pairs_kernel(factor, pairs, u_tab, s_tab, rhs, out, work):
    def block(n, _):
        def group(g, _):
            for e in range(8):
                p = n * BLOCK + g * 8 + e
                i = pl.multiple_of(pairs[2 * p] * STEP, 8)
                j = pl.multiple_of(pairs[2 * p + 1] * STEP, 8)
                for half in range(2):
                    total = None
                    for d in range(3):
                        at = half * 24 + d * 8
                        term = u_tab[pl.ds(i + at, 8), :] * s_tab[pl.ds(j + at, 8), :]
                        total = term if total is None else total + term
                    work[half, pl.ds(pl.multiple_of((g * 8 + e) * 8, 8), 8), :] = total
            return 0

        lax.fori_loop(0, BLOCK // 8, group, 0)
        highs, lows = [], []
        for half in range(2):
            for r in range(6):
                value = work[half, pl.ds(r, BLOCK, stride=8), :]
                a, b = split(value)
                highs.append(a)
                lows.append(b)
        wide = dot(jnp.concatenate(highs, axis=1), rhs[...])
        narrow = dot(jnp.concatenate(lows, axis=1), rhs[:, 0:128])
        out[pl.ds(pl.multiple_of(n * BLOCK, BLOCK), BLOCK), :] = (
            wide[:, 0:128] + (wide[:, 128:256] + narrow)
        ) * factor
        return 0

    lax.fori_loop(0, PAIRS // BLOCK, block, 0)


def pair_terms(factor, pairs, u_tab, s_tab, rhs):
    vmem = pl.BlockSpec(memory_space=pltpu.VMEM)
    return pl.pallas_call(
        functools.partial(pairs_kernel, factor),
        out_shape=jax.ShapeDtypeStruct((PAIRS, MODES), F32),
        in_specs=[pl.BlockSpec(memory_space=pltpu.SMEM), vmem, vmem, vmem],
        out_specs=vmem,
        scratch_shapes=[pltpu.VMEM((2, BLOCK * 8, LANES), F32)],
        compiler_params=pltpu.CompilerParams(vmem_limit_bytes=48 * 2**20),
        name="pairs",
    )(pairs, u_tab, s_tab, rhs)


def reduce_kernel(part, out, half, got, quarter, got_x, last, got_yz, c_s, c_r, x_s, x_r, f_s, f_r):
    x, y, zh, zl, core = here()
    tm, space = lax.axis_index("tm"), lax.axis_index("space")
    other = there(x, y, zh, zl, 1 - core)
    barrier = pltpu.get_barrier_semaphore()
    xs = [there(lax.rem(x + k, 4), y, zh, zl, core) for k in range(1, 4)]
    places = [(k % 4, (k // 4) % 2, k // 8) for k in range(16)]

    def place(k):
        dy, dl, dh = places[k]
        return lax.rem(y + dy, 4), lax.rem(zh + dh, 2), lax.rem(zl + dl, 2)

    fs = []
    for k in range(1, 16):
        ty, th, tl = place(k)
        fs.append(there(x, ty, th, tl, core))
    for target in [other, *xs, *fs]:
        pl.semaphore_signal(barrier, inc=1, device_id=target, device_id_type=MESH)
    pl.semaphore_wait(barrier, 19)

    swap = pltpu.make_async_remote_copy(
        src_ref=part.at[:, :, :, 1 - core], dst_ref=got, send_sem=c_s, recv_sem=c_r,
        device_id=other, device_id_type=MESH,
    )
    swap.start()
    swap.wait()
    for xk in range(4):
        half[xk] = part[:, xk, :, core] + got[:, xk]

    def x_copy(k):
        return pltpu.make_async_remote_copy(
            src_ref=half.at[lax.rem(x + k, 4)], dst_ref=got_x.at[k - 1],
            send_sem=x_s.at[k - 1], recv_sem=x_r.at[k - 1], device_id=xs[k - 1], device_id_type=MESH,
        )

    for k in (1, 3, 2):
        x_copy(k).start()
    for k in (1, 3, 2):
        x_copy(k).wait()
    quarter[...] = (half[x] + got_x[0]) + (got_x[1] + got_x[2])

    def f_copy(k):
        ty, th, tl = place(k)
        return pltpu.make_async_remote_copy(
            src_ref=quarter.at[th, tl * 4 + ty], dst_ref=got_yz.at[k - 1],
            send_sem=f_s.at[k - 1], recv_sem=f_r.at[k - 1], device_id=fs[k - 1], device_id_type=MESH,
        )

    for k in range(1, 16):
        f_copy(k).start()
    for k in range(1, 16):
        f_copy(k).wait()
    total = quarter[zh, zl * 4 + y]
    for k in range(15):
        total = total + got_yz[k]
    out[...] = total


def reduce_scatter(part):
    vmem = pl.BlockSpec(memory_space=pltpu.VMEM)
    dma = pltpu.SemaphoreType.DMA
    return pl.pallas_call(
        reduce_kernel,
        out_shape=jax.ShapeDtypeStruct((32, MODES), F32),
        in_specs=[vmem],
        out_specs=vmem,
        scratch_shapes=[
            pltpu.VMEM((4, 2, 8, 32, MODES), F32),
            pltpu.VMEM((2, 4, 8, 32, MODES), F32),
            pltpu.VMEM((2, 8, 32, MODES), F32),
            pltpu.VMEM((3, 2, 8, 32, MODES), F32),
            pltpu.VMEM((1, MODES), F32),
            pltpu.VMEM((15, 32, MODES), F32),
            dma, dma, dma((3,)), dma((3,)), dma((15,)), dma((15,)),
        ],
        compiler_params=pltpu.CompilerParams(
            collective_id=1, has_side_effects=True, vmem_limit_bytes=48 * 2**20
        ),
        name="reduce",
    )(part.reshape(2, 4, 8, 2, 32, MODES))


def shards(snapshots, coeffs, pair_table):
    u_tab, s_tab, rhs = make_tables(snapshots.reshape(32 * 96, LANES), coeffs)
    part = pair_terms(0.5 / 256.0, pair_table.reshape(-1), u_tab, s_tab, rhs)
    return reduce_scatter(part)


def solution(mesh):
    placed = (P("tm", None, "space", None, None), P(), P())
    return jax.shard_map(
        shards, mesh=mesh, in_specs=placed, out_specs=P(("tm", "space"), None), check_vma=False
    )
```

```python
import functools

import jax
import jax.numpy as jnp
from jax import lax
from jax.experimental import pallas as pl
from jax.experimental.pallas import tpu as pltpu
from jax.sharding import PartitionSpec as P

MESH = pl.DeviceIdType.MESH
F32 = jnp.float32
BF16 = jnp.bfloat16
MODES = 128
LANES = 128
PAIRS = 4096
STEP = 56
BLOCK = 128


def here():
    t, s = lax.axis_index("tm"), lax.axis_index("space")
    return lax.rem(t, 4), lax.rem(lax.div(s, 2), 4), lax.div(t, 4), lax.div(s, 8), lax.rem(s, 2)


def there(x, y, zh, zl, core):
    return zh * 4 + x, zl * 8 + y * 2 + core


def band_of(x, zh):
    return x + zh * (7 - 2 * x)


def owner_of(band):
    zh = lax.div(band, 4)
    return zh * 4 + band + zh * (7 - 2 * band)


def split(value):
    high = value.astype(BF16)
    return high, (value - high.astype(F32)).astype(BF16)


def dot(a, b):
    return jnp.dot(a, b, preferred_element_type=F32)


ORDER = (5, 2, 7, 4, 1, 6, 3)


def tables_kernel(
    snaps, coeffs, u_tab, s_tab, rhs, send, recv, modes, below, above, low, high,
    own_sem, a2a_s, a2a_r, x_s, x_r, y_s, y_r,
):
    x, y, zh, zl, core = here()
    tm, space = lax.axis_index("tm"), lax.axis_index("space")
    band = band_of(x, zh)
    after, before = lax.rem(space + 1, 16), lax.rem(space + 15, 16)

    def partner(rel):
        return lax.rem(zh + rel // 4, 2) * 4 + lax.rem(x + rel % 4, 4)

    barrier = pltpu.get_barrier_semaphore()
    for rel in range(1, 8):
        pl.semaphore_signal(barrier, inc=1, device_id=(partner(rel), space), device_id_type=MESH)
    for side in (after, before):
        pl.semaphore_signal(barrier, inc=1, device_id=(tm, side), device_id_type=MESH)

    for b in range(8):
        for c in range(3):
            for r in range(4):
                send[b, c * 4 + r] = snaps[pl.ds(c * 32 + 4 * b + r, 32, stride=96), :]
    own = pltpu.make_async_copy(send.at[band], recv.at[:, pl.ds(tm * 32, 32), :], own_sem)
    own.start()
    pl.semaphore_wait(barrier, 9)

    def exchange(c, rel):
        t = partner(rel)
        zt, xt = lax.div(t, 4), lax.rem(t, 4)
        return pltpu.make_async_remote_copy(
            src_ref=send.at[band_of(xt, zt), pl.ds(c * 4, 4)],
            dst_ref=recv.at[pl.ds(c * 4, 4), pl.ds(tm * 32, 32), :],
            send_sem=a2a_s.at[c, rel], recv_sem=a2a_r.at[c, rel],
            device_id=(t, space), device_id_type=MESH,
        )

    def x_copy(c, up):
        return pltpu.make_async_remote_copy(
            src_ref=modes.at[pl.ds(c * 4, 4)],
            dst_ref=(below if up else above).at[pl.ds(c * 4, 4)],
            send_sem=x_s.at[c, up], recv_sem=x_r.at[c, up],
            device_id=(tm, after if up else before), device_id_type=MESH,
        )

    def y_copy(c, up):
        target = owner_of(jnp.minimum(band + 1, 7) if up else jnp.maximum(band - 1, 0))
        return pltpu.make_async_remote_copy(
            src_ref=modes.at[c * 4 + (3 if up else 0)],
            dst_ref=(low if up else high).at[c],
            send_sem=y_s.at[c, up], recv_sem=y_r.at[c, up],
            device_id=(target, space), device_id_type=MESH,
        )

    for c in range(3):
        for rel in ORDER:
            exchange(c, rel).start()

    @pl.when(band == 0)
    def _():
        low[...] = jnp.zeros_like(low)

    @pl.when(band == 7)
    def _():
        high[...] = jnp.zeros_like(high)

    coeff_high, coeff_low = split(coeffs[...].T)
    own.wait()
    for c in range(3):
        for rel in ORDER:
            exchange(c, rel).wait_recv()
        rows = jnp.concatenate([recv[c * 4 + r] for r in range(4)], axis=1)
        row_high, row_low = split(rows)
        field = dot(coeff_high, row_high) + dot(coeff_high, row_low) + dot(coeff_low, row_high)
        for r in range(4):
            modes[c * 4 + r] = field[:, r * 128 : r * 128 + 128]
        for up in (1, 0):
            x_copy(c, up).start()

        @pl.when(band < 7)
        def _():
            y_copy(c, 1).start()

        @pl.when(band > 0)
        def _():
            y_copy(c, 0).start()

        for r in range(4):
            half, row = r // 2, r % 2
            value = field[:, r * 128 : r * 128 + 128]
            slot = half * 24 + c * 8 + row
            for copy in range(3):
                u_tab[pl.ds(slot + 2 * copy, MODES, stride=STEP), :] = value
            turned_high, turned_low = split(value.T)
            at = (half * 6 + c * 2 + row) * LANES
            rhs[at : at + LANES, 0:128] = turned_high
            rhs[at : at + LANES, 128:256] = turned_low
            slope = pltpu.roll(value, 127, 1) - pltpu.roll(value, 1, 1)
            s_tab[pl.ds(half * 24 + 16 + c * 2 + row, MODES, stride=STEP), :] = slope

    for c in range(3):
        @pl.when(band > 0)
        def _():
            y_copy(c, 1).wait_recv()

        @pl.when(band < 7)
        def _():
            y_copy(c, 0).wait_recv()

        for r in range(4):
            half, row = r // 2, r % 2
            under = low[c] if r == 0 else modes[c * 4 + r - 1]
            over = high[c] if r == 3 else modes[c * 4 + r + 1]
            s_tab[pl.ds(half * 24 + 8 + c * 2 + row, MODES, stride=STEP), :] = over - under
        for up in (1, 0):
            x_copy(c, up).wait_recv()
        for r in range(4):
            half, row = r // 2, r % 2
            slope = above[c * 4 + r] - below[c * 4 + r]
            s_tab[pl.ds(half * 24 + c * 2 + row, MODES, stride=STEP), :] = slope

    for c in range(3):
        for rel in ORDER:
            exchange(c, rel).wait_send()
        for up in (1, 0):
            x_copy(c, up).wait_send()

        @pl.when(band < 7)
        def _():
            y_copy(c, 1).wait_send()

        @pl.when(band > 0)
        def _():
            y_copy(c, 0).wait_send()


def make_tables(snaps, coeffs):
    vmem = pl.BlockSpec(memory_space=pltpu.VMEM)
    dma = pltpu.SemaphoreType.DMA
    return pl.pallas_call(
        tables_kernel,
        out_shape=[
            jax.ShapeDtypeStruct((MODES * STEP, LANES), F32),
            jax.ShapeDtypeStruct((MODES * STEP, LANES), F32),
            jax.ShapeDtypeStruct((12 * LANES, 256), BF16),
        ],
        in_specs=[vmem, vmem],
        out_specs=[vmem, vmem, vmem],
        scratch_shapes=[
            pltpu.VMEM((8, 12, 32, LANES), F32),
            pltpu.VMEM((12, 256, LANES), F32),
            pltpu.VMEM((12, MODES, LANES), F32),
            pltpu.VMEM((12, MODES, LANES), F32),
            pltpu.VMEM((12, MODES, LANES), F32),
            pltpu.VMEM((3, MODES, LANES), F32),
            pltpu.VMEM((3, MODES, LANES), F32),
            dma, dma((3, 8)), dma((3, 8)), dma((3, 2)), dma((3, 2)), dma((3, 2)), dma((3, 2)),
        ],
        compiler_params=pltpu.CompilerParams(
            collective_id=0, has_side_effects=True, vmem_limit_bytes=24 * 2**20
        ),
        name="tables",
    )(snaps, coeffs)


AXES = (0, 1, 2, 0)
CHUNKS = 4
PER_CHUNK = PAIRS // CHUNKS // BLOCK


def flat(units, axis):
    rest = [units[k] for k in range(3) if k != axis]
    return units[axis], rest[0] * 4 + rest[1]


def pairs_kernel(
    factor, pairs, u_tab, s_tab, rhs, out,
    work_a, work_b, part, got, half, got_a, quarter, got_b,
    c_s, c_r, a_s, a_r, b_s, b_r,
):
    x, y, zh, zl, core = here()
    z = zh * 2 + zl
    barrier = pltpu.get_barrier_semaphore()

    def device(tx, ty, tz, tc):
        return there(tx, ty, lax.div(tz, 2), lax.rem(tz, 2), tc)

    def moved(steps):
        return tuple(lax.rem(a + b, 4) if b else a for a, b in zip((x, y, z), steps))

    def line(axis, k):
        return moved(tuple(k if n == axis else 0 for n in range(3)))

    def plane(axis, k):
        steps = [k // 4, k % 4]
        return moved(tuple(0 if n == axis else steps.pop(0) for n in range(3)))

    targets = [device(x, y, z, 1 - core)]
    for axis in sorted(set(AXES)):
        for k in range(1, 16):
            targets.append(device(*plane(axis, k), core))
    for n in range(len(targets)):
        pl.semaphore_signal(barrier, inc=1, device_id=targets[n], device_id_type=MESH)

    def gather(n, work):
        q, d0 = lax.div(n, PER_CHUNK), lax.rem(n, PER_CHUNK) * (BLOCK // 8)
        numbers = pairs.at[pl.ds(pl.multiple_of(d0 * 64 + q * 8, 8), BLOCK * 8 - 24)]
        for e in range(BLOCK):
            at = (e // 32) * 256 + (e // 8 % 4) * 32 + e % 8
            i, j = numbers[at], numbers[at + 128]
            for h in range(2):
                total = None
                for d in range(3):
                    row = h * 24 + d * 8
                    term = u_tab[i, row : row + 8, :] * s_tab[j, row : row + 8, :]
                    total = term if total is None else total + term
                work[(h * BLOCK + e) * 9 : (h * BLOCK + e) * 9 + 8, :] = total

    def project(n, work):
        highs, lows = [], []
        for h in range(2):
            for r in range(6):
                a, b = split(work[pl.ds(h * BLOCK * 9 + r, BLOCK, stride=9), :])
                highs.append(a)
                lows.append(b)
        wide = dot(jnp.concatenate(highs, axis=1), rhs[...])
        narrow = dot(jnp.concatenate(lows, axis=1), rhs[:, 0:128])
        value = (wide[:, 0:128] + (wide[:, 128:256] + narrow)) * factor
        q, d0 = lax.div(n, PER_CHUNK), lax.rem(n, PER_CHUNK) * (BLOCK // 16)
        for u in range(BLOCK // 16):
            for c in range(2):
                part[q, c, d0 + u] = value[(2 * u + c) * 8 : (2 * u + c) * 8 + 8, :]

    def c_copy(q):
        return pltpu.make_async_remote_copy(
            src_ref=part.at[q, 1 - core], dst_ref=got.at[q], send_sem=c_s.at[q], recv_sem=c_r.at[q],
            device_id=device(x, y, z, 1 - core), device_id_type=MESH,
        )

    def a_copy(q, k):
        to = line(AXES[q], k)
        return pltpu.make_async_remote_copy(
            src_ref=half.at[q, to[AXES[q]]], dst_ref=got_a.at[q, k - 1],
            send_sem=a_s.at[q, k - 1], recv_sem=a_r.at[q, k - 1],
            device_id=device(*to, core), device_id_type=MESH,
        )

    def b_copy(q, k):
        to = plane(AXES[q], k)
        return pltpu.make_async_remote_copy(
            src_ref=quarter.at[q, flat(to, AXES[q])[1]], dst_ref=got_b.at[q, k - 1],
            send_sem=b_s.at[q, k - 1], recv_sem=b_r.at[q, k - 1],
            device_id=device(*to, core), device_id_type=MESH,
        )

    def stage_c(q):
        c_copy(q).start()

    def stage_a(q):
        c_copy(q).wait_recv()
        for u in range(64):
            tzh, tx, tzl, ty = u // 32, (u // 8) % 4, (u // 4) % 2, u % 4
            a, b = flat((tx, ty, tzh * 2 + tzl), AXES[q])
            half[q, a, b] = part[q, core, u] + got[q, u]
        for k in (1, 3, 2):
            a_copy(q, k).start()

    def stage_b(q):
        for k in (1, 3, 2):
            a_copy(q, k).wait_recv()
        mine = half[q, (x, y, z)[AXES[q]]]
        quarter[q] = (mine + got_a[q, 0]) + (got_a[q, 1] + got_a[q, 2])
        for k in range(1, 16):
            b_copy(q, k).start()

    def stage_d(q):
        for k in range(1, 16):
            b_copy(q, k).wait_recv()
        total = quarter[q, flat((x, y, z), AXES[q])[1]]
        for k in range(15):
            total = total + got_b[q, k]
        out[q * 8 : q * 8 + 8, :] = total

    def greet():
        pl.semaphore_wait(barrier, len(targets))

    trips = CHUNKS * PER_CHUNK
    stages = {
        2: [greet, (stage_c, 0)], 3: [(stage_a, 0)], 4: [(stage_c, 1)], 5: [(stage_a, 1), (stage_b, 0)],
        6: [(stage_c, 2)], 7: [(stage_a, 2), (stage_b, 1), (stage_d, 0)],
    }

    def trip(m, _):
        for parity, (now, later) in enumerate(((work_a, work_b), (work_b, work_a))):
            @pl.when(lax.rem(m, 2) == parity)
            def _():
                gather(jnp.minimum(m + 1, trips - 1), later)
                project(m, now)

        for t, todo in stages.items():
            @pl.when(m == t * trips // 8 - 1)
            def _():
                for item in todo:
                    if callable(item):
                        item()
                    else:
                        item[0](item[1])
        return 0

    gather(0, work_a)
    lax.fori_loop(0, trips, trip, 0)
    for stage, q in (
        (stage_c, 3), (stage_b, 2), (stage_a, 3), (stage_d, 1), (stage_d, 2), (stage_b, 3), (stage_d, 3),
    ):
        stage(q)
    for q in range(CHUNKS):
        c_copy(q).wait_send()
        for k in range(1, 4):
            a_copy(q, k).wait_send()
        for k in range(1, 16):
            b_copy(q, k).wait_send()


def pair_terms(factor, pairs, u_tab, s_tab, rhs):
    vmem = pl.BlockSpec(memory_space=pltpu.VMEM)
    dma = pltpu.SemaphoreType.DMA
    tile = (8, MODES)
    return pl.pallas_call(
        functools.partial(pairs_kernel, factor),
        out_shape=jax.ShapeDtypeStruct((32, MODES), F32),
        in_specs=[pl.BlockSpec(memory_space=pltpu.SMEM), vmem, vmem, vmem],
        out_specs=vmem,
        scratch_shapes=[
            pltpu.VMEM((2 * BLOCK * 9 + 8, LANES), F32),
            pltpu.VMEM((2 * BLOCK * 9 + 8, LANES), F32),
            pltpu.VMEM((CHUNKS, 2, 64, *tile), F32),
            pltpu.VMEM((CHUNKS, 64, *tile), F32),
            pltpu.VMEM((CHUNKS, 4, 16, *tile), F32),
            pltpu.VMEM((CHUNKS, 3, 16, *tile), F32),
            pltpu.VMEM((CHUNKS, 16, *tile), F32),
            pltpu.VMEM((CHUNKS, 15, *tile), F32),
            dma((CHUNKS,)), dma((CHUNKS,)), dma((CHUNKS, 3)), dma((CHUNKS, 3)),
            dma((CHUNKS, 15)), dma((CHUNKS, 15)),
        ],
        compiler_params=pltpu.CompilerParams(
            collective_id=1, has_side_effects=True, vmem_limit_bytes=24 * 2**20
        ),
        name="pairs",
    )(pairs, u_tab, s_tab, rhs)


def shards(snapshots, coeffs, pair_table):
    u_tab, s_tab, rhs = make_tables(snapshots.reshape(32 * 96, LANES), coeffs)
    u_tab, s_tab = (t.reshape(MODES, STEP, LANES) for t in (u_tab, s_tab))
    return pair_terms(0.5 / 256.0, pair_table.reshape(32, 128, 2).transpose(0, 2, 1).reshape(-1), u_tab, s_tab, rhs)


def solution(mesh):
    placed = (P("tm", None, "space", None, None), P(), P())
    return jax.shard_map(
        shards, mesh=mesh, in_specs=placed, out_specs=P(("tm", "space"), None), check_vma=False
    )
```

```python
import functools

import jax
import jax.numpy as jnp
from jax import lax
from jax.experimental import pallas as pl
from jax.experimental.pallas import tpu as pltpu
from jax.sharding import PartitionSpec as P

MESH = pl.DeviceIdType.MESH
F32 = jnp.float32
BF16 = jnp.bfloat16
MODES = 128
LANES = 128
PAIRS = 4096
STEP = 56
BLOCK = 128


def here():
    t, s = lax.axis_index("tm"), lax.axis_index("space")
    return lax.rem(t, 4), lax.rem(lax.div(s, 2), 4), lax.div(t, 4), lax.div(s, 8), lax.rem(s, 2)


def there(x, y, zh, zl, core):
    return zh * 4 + x, zl * 8 + y * 2 + core


def band_of(x, zh):
    return x + zh * (7 - 2 * x)


def owner_of(band):
    zh = lax.div(band, 4)
    return zh * 4 + band + zh * (7 - 2 * band)


def split(value):
    high = value.astype(BF16)
    return high, (value - high.astype(F32)).astype(BF16)


def dot(a, b):
    return jnp.dot(a, b, preferred_element_type=F32)


ORDER = (5, 2, 7, 4, 1, 6, 3)


def tables_kernel(
    snaps, coeffs, u_tab, s_tab, rhs, send, recv, modes, below, above, low, high,
    own_sem, a2a_s, a2a_r, x_s, x_r, y_s, y_r,
):
    x, y, zh, zl, core = here()
    tm, space = lax.axis_index("tm"), lax.axis_index("space")
    band = band_of(x, zh)
    after, before = lax.rem(space + 1, 16), lax.rem(space + 15, 16)

    def partner(rel):
        return lax.rem(zh + rel // 4, 2) * 4 + lax.rem(x + rel % 4, 4)

    barrier = pltpu.get_barrier_semaphore()
    for rel in range(1, 8):
        pl.semaphore_signal(barrier, inc=1, device_id=(partner(rel), space), device_id_type=MESH)
    for side in (after, before):
        pl.semaphore_signal(barrier, inc=1, device_id=(tm, side), device_id_type=MESH)

    for b in range(8):
        for c in range(3):
            for r in range(4):
                send[b, c * 4 + r] = snaps[pl.ds(c * 32 + 4 * b + r, 32, stride=96), :]
    own = pltpu.make_async_copy(send.at[band], recv.at[:, pl.ds(tm * 32, 32), :], own_sem)
    own.start()
    pl.semaphore_wait(barrier, 9)

    def exchange(c, rel):
        t = partner(rel)
        zt, xt = lax.div(t, 4), lax.rem(t, 4)
        return pltpu.make_async_remote_copy(
            src_ref=send.at[band_of(xt, zt), pl.ds(c * 4, 4)],
            dst_ref=recv.at[pl.ds(c * 4, 4), pl.ds(tm * 32, 32), :],
            send_sem=a2a_s.at[c, rel], recv_sem=a2a_r.at[c, rel],
            device_id=(t, space), device_id_type=MESH,
        )

    def x_copy(c, up):
        return pltpu.make_async_remote_copy(
            src_ref=modes.at[pl.ds(c * 4, 4)],
            dst_ref=(below if up else above).at[pl.ds(c * 4, 4)],
            send_sem=x_s.at[c, up], recv_sem=x_r.at[c, up],
            device_id=(tm, after if up else before), device_id_type=MESH,
        )

    def y_copy(c, up):
        target = owner_of(jnp.minimum(band + 1, 7) if up else jnp.maximum(band - 1, 0))
        return pltpu.make_async_remote_copy(
            src_ref=modes.at[c * 4 + (3 if up else 0)],
            dst_ref=(low if up else high).at[c],
            send_sem=y_s.at[c, up], recv_sem=y_r.at[c, up],
            device_id=(target, space), device_id_type=MESH,
        )

    for c in range(3):
        for rel in ORDER:
            exchange(c, rel).start()

    @pl.when(band == 0)
    def _():
        low[...] = jnp.zeros_like(low)

    @pl.when(band == 7)
    def _():
        high[...] = jnp.zeros_like(high)

    coeff_high, coeff_low = split(coeffs[...].T)
    own.wait()
    for c in range(3):
        for rel in ORDER:
            exchange(c, rel).wait_recv()
        rows = jnp.concatenate([recv[c * 4 + r] for r in range(4)], axis=1)
        row_high, row_low = split(rows)
        field = dot(coeff_high, row_high) + dot(coeff_high, row_low) + dot(coeff_low, row_high)
        for r in range(4):
            modes[c * 4 + r] = field[:, r * 128 : r * 128 + 128]
        for up in (1, 0):
            x_copy(c, up).start()

        @pl.when(band < 7)
        def _():
            y_copy(c, 1).start()

        @pl.when(band > 0)
        def _():
            y_copy(c, 0).start()

        for r in range(4):
            half, row = r // 2, r % 2
            value = field[:, r * 128 : r * 128 + 128]
            slot = half * 24 + c * 8 + row
            for copy in range(3):
                u_tab[pl.ds(slot + 2 * copy, MODES, stride=STEP), :] = value
            turned_high, turned_low = split(value.T)
            at = (half * 6 + c * 2 + row) * LANES
            rhs[at : at + LANES, 0:128] = turned_high
            rhs[at : at + LANES, 128:256] = turned_low
            slope = pltpu.roll(value, 127, 1) - pltpu.roll(value, 1, 1)
            s_tab[pl.ds(half * 24 + 16 + c * 2 + row, MODES, stride=STEP), :] = slope

    for c in range(3):
        @pl.when(band > 0)
        def _():
            y_copy(c, 1).wait_recv()

        @pl.when(band < 7)
        def _():
            y_copy(c, 0).wait_recv()

        for r in range(4):
            half, row = r // 2, r % 2
            under = low[c] if r == 0 else modes[c * 4 + r - 1]
            over = high[c] if r == 3 else modes[c * 4 + r + 1]
            s_tab[pl.ds(half * 24 + 8 + c * 2 + row, MODES, stride=STEP), :] = over - under
        for up in (1, 0):
            x_copy(c, up).wait_recv()
        for r in range(4):
            half, row = r // 2, r % 2
            slope = above[c * 4 + r] - below[c * 4 + r]
            s_tab[pl.ds(half * 24 + c * 2 + row, MODES, stride=STEP), :] = slope

    for c in range(3):
        for rel in ORDER:
            exchange(c, rel).wait_send()
        for up in (1, 0):
            x_copy(c, up).wait_send()

        @pl.when(band < 7)
        def _():
            y_copy(c, 1).wait_send()

        @pl.when(band > 0)
        def _():
            y_copy(c, 0).wait_send()


def make_tables(snaps, coeffs):
    vmem = pl.BlockSpec(memory_space=pltpu.VMEM)
    dma = pltpu.SemaphoreType.DMA
    return pl.pallas_call(
        tables_kernel,
        out_shape=[
            jax.ShapeDtypeStruct((MODES * STEP, LANES), F32),
            jax.ShapeDtypeStruct((MODES * STEP, LANES), F32),
            jax.ShapeDtypeStruct((12 * LANES, 256), BF16),
        ],
        in_specs=[vmem, vmem],
        out_specs=[vmem, vmem, vmem],
        scratch_shapes=[
            pltpu.VMEM((8, 12, 32, LANES), F32),
            pltpu.VMEM((12, 256, LANES), F32),
            pltpu.VMEM((12, MODES, LANES), F32),
            pltpu.VMEM((12, MODES, LANES), F32),
            pltpu.VMEM((12, MODES, LANES), F32),
            pltpu.VMEM((3, MODES, LANES), F32),
            pltpu.VMEM((3, MODES, LANES), F32),
            dma, dma((3, 8)), dma((3, 8)), dma((3, 2)), dma((3, 2)), dma((3, 2)), dma((3, 2)),
        ],
        compiler_params=pltpu.CompilerParams(
            collective_id=0, has_side_effects=True, vmem_limit_bytes=24 * 2**20
        ),
        name="tables",
    )(snaps, coeffs)


PIECES = 16
FAR = 12
CUTS = (0, 16, 36, 56, 76, 96, 128)


def pairs_kernel(
    factor, pairs, u_tab, s_tab, rhs, out,
    work_a, work_b, part, got, half, got_x, own, got_y, got_z,
    c_s, c_r, x_s, x_r, y_s, y_r, z_s, z_r,
):
    x, y, zh, zl, core = here()
    z = zh * 2 + zl
    barrier = pltpu.get_barrier_semaphore()

    def device(dx=0, dy=0, dz=0, flip=0):
        tz = lax.rem(z + dz, 4)
        tx, ty = lax.rem(x + dx, 4), lax.rem(y + dy, 4)
        return there(tx, ty, lax.div(tz, 2), lax.rem(tz, 2), 1 - core if flip else core)

    targets = [device(flip=1)]
    for k in range(1, 4):
        targets += [device(dx=k), device(dy=k), device(dz=k)]
    for target in targets:
        pl.semaphore_signal(barrier, inc=1, device_id=target, device_id_type=MESH)

    def steps(k):
        far = k < FAR
        r = lax.rem(k, 3)
        dx = jnp.where(far, 1 + 2 * r - 3 * lax.div(r, 2), 0)
        return dx, lax.rem(jnp.where(far, lax.div(k, 3), k - FAR) + 1, 4)

    def gather(n, work, low, high):
        k, wh = lax.div(n, 2), lax.rem(n, 2)
        dx, dy = steps(k)
        tx, ty = lax.rem(x + dx, 4), lax.rem(y + dy, 4)
        base = (wh * 16 + tx * 4 + lax.div(ty, 2)) * 256 + lax.rem(ty, 2) * 64
        numbers = pairs.at[pl.ds(pl.multiple_of(base, 8), 704)]
        for e in range(low, high):
            at = (e // 64) * 512 + e % 64
            i, j = numbers[at], numbers[at + 128]
            for h in range(2):
                total = None
                for d in range(3):
                    row = h * 24 + d * 8
                    term = u_tab[i, row : row + 8, :] * s_tab[j, row : row + 8, :]
                    total = term if total is None else total + term
                work[(h * BLOCK + e) * 9 : (h * BLOCK + e) * 9 + 8, :] = total

    def project(n, now, later):
        nxt = jnp.minimum(n + 1, 2 * PIECES - 1)
        value = None
        for t in range(6):
            h, r = t // 3, t % 3 * 2
            parts = [split(now[pl.ds(h * BLOCK * 9 + r + k, BLOCK, stride=9), :]) for k in range(2)]
            high, low = (jnp.concatenate([p[k] for p in parts], axis=1) for k in range(2))
            wide = dot(high, rhs[t * 256 : t * 256 + 256, :])
            narrow = dot(low, rhs[t * 256 : t * 256 + 256, 0:128])
            term = wide[:, 0:128] + (wide[:, 128:256] + narrow)
            value = term if value is None else value + term
            gather(nxt, later, CUTS[t], CUTS[t + 1])
        value = value * factor
        k, wh = lax.div(n, 2), lax.rem(n, 2)
        for u in range(2):
            for c in range(2):
                part[k, c, wh * 2 + u] = value[(2 * u + c) * 32 : (2 * u + c) * 32 + 32, :]

    def c_copy(k):
        return pltpu.make_async_remote_copy(
            src_ref=part.at[k, 1 - core], dst_ref=got.at[k], send_sem=c_s.at[k], recv_sem=c_r.at[k],
            device_id=device(flip=1), device_id_type=MESH,
        )

    def x_copy(k):
        return pltpu.make_async_remote_copy(
            src_ref=half.at[k], dst_ref=got_x.at[k], send_sem=x_s.at[k], recv_sem=x_r.at[k],
            device_id=device(dx=steps(k)[0]), device_id_type=MESH,
        )

    def y_copy(o):
        return pltpu.make_async_remote_copy(
            src_ref=own.at[o], dst_ref=got_y.at[o], send_sem=y_s.at[o], recv_sem=y_r.at[o],
            device_id=device(dy=o + 1), device_id_type=MESH,
        )

    def z_copy(o):
        return pltpu.make_async_remote_copy(
            src_ref=own.at[3, lax.rem(z + o + 1, 4)], dst_ref=got_z.at[o],
            send_sem=z_s.at[o], recv_sem=z_r.at[o], device_id=device(dz=o + 1), device_id_type=MESH,
        )

    def far_piece(k):
        c_copy(k).wait_recv()
        half[k] = part[k, core] + got[k]
        x_copy(k).start()

    def near_piece(o):
        c_copy(FAR + o).wait_recv()
        for r in range(3):
            x_copy(3 * o + r).wait_recv()
        total = (part[FAR + o, core] + got[FAR + o]) + (got_x[3 * o] + (got_x[3 * o + 1] + got_x[3 * o + 2]))
        return total

    def trip(m, _):
        for parity, (now, later) in enumerate(((work_a, work_b), (work_b, work_a))):
            @pl.when(lax.rem(m, 2) == parity)
            def _():
                project(m, now, later)

        @pl.when(m == 1)
        def _():
            pl.semaphore_wait(barrier, len(targets))

        k = lax.div(m, 2)

        @pl.when(lax.rem(m, 2) == 1)
        def _():
            c_copy(k).start()

        @pl.when((lax.rem(m, 2) == 1) & (k > 0) & (k <= FAR))
        def _():
            far_piece(k - 1)

        return 0

    gather(0, work_a, 0, BLOCK)
    lax.fori_loop(0, 2 * PIECES, trip, 0)
    for o in range(3):
        own[o] = near_piece(o)
        y_copy(o).start()
    total = near_piece(3)
    for o in range(3):
        y_copy(o).wait_recv()
    own[3] = total + (got_y[0] + (got_y[1] + got_y[2]))
    for o in (0, 2, 1):
        z_copy(o).start()
    for o in range(3):
        z_copy(o).wait_recv()
    out[...] = own[3, z] + (got_z[0] + (got_z[1] + got_z[2]))
    for k in range(PIECES):
        c_copy(k).wait_send()
    for k in range(FAR):
        x_copy(k).wait_send()
    for o in range(3):
        y_copy(o).wait_send()
        z_copy(o).wait_send()


def pair_terms(factor, pairs, u_tab, s_tab, rhs):
    vmem = pl.BlockSpec(memory_space=pltpu.VMEM)
    dma = pltpu.SemaphoreType.DMA
    piece = (4, 32, MODES)
    return pl.pallas_call(
        functools.partial(pairs_kernel, factor),
        out_shape=jax.ShapeDtypeStruct((32, MODES), F32),
        in_specs=[pl.BlockSpec(memory_space=pltpu.SMEM), vmem, vmem, vmem],
        out_specs=vmem,
        scratch_shapes=[
            pltpu.VMEM((2 * BLOCK * 9 + 8, LANES), F32),
            pltpu.VMEM((2 * BLOCK * 9 + 8, LANES), F32),
            pltpu.VMEM((PIECES, 2, *piece), F32),
            pltpu.VMEM((PIECES, *piece), F32),
            pltpu.VMEM((FAR, *piece), F32),
            pltpu.VMEM((FAR, *piece), F32),
            pltpu.VMEM((4, *piece), F32),
            pltpu.VMEM((3, *piece), F32),
            pltpu.VMEM((3, 32, MODES), F32),
            dma((PIECES,)), dma((PIECES,)), dma((FAR,)), dma((FAR,)),
            dma((3,)), dma((3,)), dma((3,)), dma((3,)),
        ],
        compiler_params=pltpu.CompilerParams(
            collective_id=1, has_side_effects=True, vmem_limit_bytes=24 * 2**20
        ),
        name="pairs",
    )(pairs, u_tab, s_tab, rhs)


def shards(snapshots, coeffs, pair_table):
    u_tab, s_tab, rhs = make_tables(snapshots.reshape(32 * 96, LANES), coeffs)
    u_tab, s_tab = (t.reshape(MODES, STEP, LANES) for t in (u_tab, s_tab))
    return pair_terms(0.5 / 256.0, pair_table.reshape(32, 128, 2).transpose(0, 2, 1).reshape(-1), u_tab, s_tab, rhs)


def solution(mesh):
    placed = (P("tm", None, "space", None, None), P(), P())
    return jax.shard_map(
        shards, mesh=mesh, in_specs=placed, out_specs=P(("tm", "space"), None), check_vma=False
    )
```

```python
import functools

import jax
import jax.numpy as jnp
from jax import lax
from jax.experimental import pallas as pl
from jax.experimental.pallas import tpu as pltpu
from jax.sharding import PartitionSpec as P

MESH = pl.DeviceIdType.MESH
F32 = jnp.float32
BF16 = jnp.bfloat16
MODES = 128
LANES = 128
PAIRS = 4096
STEP = 56
BLOCK = 128


def here():
    t, s = lax.axis_index("tm"), lax.axis_index("space")
    return lax.rem(t, 4), lax.rem(lax.div(s, 2), 4), lax.div(t, 4), lax.div(s, 8), lax.rem(s, 2)


def there(x, y, zh, zl, core):
    return zh * 4 + x, zl * 8 + y * 2 + core


def band_of(x, zh):
    return x + zh * (7 - 2 * x)


def owner_of(band):
    zh = lax.div(band, 4)
    return zh * 4 + band + zh * (7 - 2 * band)


def split(value):
    high = value.astype(BF16)
    return high, (value - high.astype(F32)).astype(BF16)


def dot(a, b):
    return jnp.dot(a, b, preferred_element_type=F32)


ORDER = (5, 2, 7, 4, 1, 6, 3)
SPANS = ((0, 5), (5, 9), (9, 12))


def tables_kernel(
    others, snaps_hbm, coeffs_hbm, u_tab, s_tab, rhs, snaps, coeffs, send, recv, modes, below, above, low, high,
    in_sem, own_sem, a2a_s, a2a_r, x_s, x_r, y_s, y_r,
):
    x, y, zh, zl, core = here()
    tm, space = lax.axis_index("tm"), lax.axis_index("space")
    band = band_of(x, zh)
    after, before = lax.rem(space + 1, 16), lax.rem(space + 15, 16)
    loads = [
        pltpu.make_async_copy(snaps_hbm, snaps, in_sem.at[0]),
        pltpu.make_async_copy(coeffs_hbm, coeffs, in_sem.at[1]),
    ]
    for load in loads:
        load.start()

    def partner(rel):
        return lax.rem(zh + rel // 4, 2) * 4 + lax.rem(x + rel % 4, 4)

    barrier = pltpu.get_barrier_semaphore()
    for rel in range(1, 8):
        pl.semaphore_signal(barrier, inc=1, device_id=(partner(rel), space), device_id_type=MESH)
    for side in (after, before):
        pl.semaphore_signal(barrier, inc=1, device_id=(tm, side), device_id_type=MESH)
    for target in others:
        pl.semaphore_signal(barrier, inc=1, device_id=target, device_id_type=MESH)

    loads[0].wait()
    for b in range(8):
        for c in range(3):
            for r in range(4):
                send[b, c * 4 + r] = snaps[pl.ds(c * 32 + 4 * b + r, 32, stride=96), :]
    own = pltpu.make_async_copy(send.at[band], recv.at[:, pl.ds(tm * 32, 32), :], own_sem)
    own.start()
    pl.semaphore_wait(barrier, 9 + len(others))

    def exchange(g, rel):
        first, last = SPANS[g]
        t = partner(rel)
        zt, xt = lax.div(t, 4), lax.rem(t, 4)
        return pltpu.make_async_remote_copy(
            src_ref=send.at[band_of(xt, zt), pl.ds(first, last - first)],
            dst_ref=recv.at[pl.ds(first, last - first), pl.ds(tm * 32, 32), :],
            send_sem=a2a_s.at[g, rel], recv_sem=a2a_r.at[g, rel],
            device_id=(t, space), device_id_type=MESH,
        )

    def x_copy(g, up):
        first, last = SPANS[g]
        return pltpu.make_async_remote_copy(
            src_ref=modes.at[pl.ds(first, last - first)],
            dst_ref=(below if up else above).at[pl.ds(first, last - first)],
            send_sem=x_s.at[g, up], recv_sem=x_r.at[g, up],
            device_id=(tm, after if up else before), device_id_type=MESH,
        )

    def y_copy(c, up):
        target = owner_of(jnp.minimum(band + 1, 7) if up else jnp.maximum(band - 1, 0))
        return pltpu.make_async_remote_copy(
            src_ref=modes.at[c * 4 + (3 if up else 0)],
            dst_ref=(low if up else high).at[c],
            send_sem=y_s.at[c, up], recv_sem=y_r.at[c, up],
            device_id=(target, space), device_id_type=MESH,
        )

    for g in range(len(SPANS)):
        for rel in ORDER:
            exchange(g, rel).start()

    @pl.when(band == 0)
    def _():
        low[...] = jnp.zeros_like(low)

    @pl.when(band == 7)
    def _():
        high[...] = jnp.zeros_like(high)

    loads[1].wait()
    coeff_high, coeff_low = split(coeffs[...].T)
    own.wait()

    def place(row):
        c, r = row // 4, row % 4
        return c, r, r // 2 * 24 + r % 2

    for g, (first, last) in enumerate(SPANS):
        for rel in ORDER:
            exchange(g, rel).wait_recv()
        rows = jnp.concatenate([recv[row] for row in range(first, last)], axis=1)
        row_high, row_low = split(rows)
        field = dot(coeff_high, row_high) + dot(coeff_high, row_low) + dot(coeff_low, row_high)
        for row in range(first, last):
            modes[row] = field[:, (row - first) * 128 : (row - first) * 128 + 128]
        for up in (1, 0):
            x_copy(g, up).start()
        for row in range(first, last):
            c, r, _ = place(row)
            if r == 3:
                @pl.when(band < 7)
                def _():
                    y_copy(c, 1).start()
            if r == 0:
                @pl.when(band > 0)
                def _():
                    y_copy(c, 0).start()

        for row in range(first, last):
            c, r, slot = place(row)
            value = field[:, (row - first) * 128 : (row - first) * 128 + 128]
            for copy in range(3):
                u_tab[pl.ds(slot + c * 8 + 2 * copy, MODES, stride=STEP), :] = value
            turned_high, turned_low = split(value.T)
            at = (r // 2 * 6 + c * 2 + r % 2) * LANES
            rhs[at : at + LANES, 0:128] = turned_high
            rhs[at : at + LANES, 128:256] = turned_low
            slope = pltpu.roll(value, 127, 1) - pltpu.roll(value, 1, 1)
            s_tab[pl.ds(slot + 16 + c * 2, MODES, stride=STEP), :] = slope

    for row in range(12):
        c, r, slot = place(row)
        if r in (1, 2):
            s_tab[pl.ds(slot + 8 + c * 2, MODES, stride=STEP), :] = modes[row + 1] - modes[row - 1]
    for g, (first, last) in enumerate(SPANS):
        for row in range(first, last):
            c, r, slot = place(row)
            if r == 0:
                @pl.when(band > 0)
                def _():
                    y_copy(c, 1).wait_recv()
                s_tab[pl.ds(slot + 8 + c * 2, MODES, stride=STEP), :] = modes[row + 1] - low[c]
            if r == 3:
                @pl.when(band < 7)
                def _():
                    y_copy(c, 0).wait_recv()
                s_tab[pl.ds(slot + 8 + c * 2, MODES, stride=STEP), :] = high[c] - modes[row - 1]
        for up in (1, 0):
            x_copy(g, up).wait_recv()
        for row in range(first, last):
            c, r, slot = place(row)
            s_tab[pl.ds(slot + c * 2, MODES, stride=STEP), :] = above[row] - below[row]

    for c in range(3):
        for rel in ORDER:
            exchange(c, rel).wait_send()
        for up in (1, 0):
            x_copy(c, up).wait_send()

        @pl.when(band < 7)
        def _():
            y_copy(c, 1).wait_send()

        @pl.when(band > 0)
        def _():
            y_copy(c, 0).wait_send()


def device(dx=0, dy=0, dz=0, flip=0):
    x, y, zh, zl, core = here()
    tz = lax.rem(zh * 2 + zl + dz, 4)
    tx, ty = lax.rem(x + dx, 4), lax.rem(y + dy, 4)
    return there(tx, ty, lax.div(tz, 2), lax.rem(tz, 2), 1 - core if flip else core)


PIECES = 16
FAR = 12
CUTS = (0, 16, 36, 56, 76, 96, 128)


def pairs_kernel(
    factor, pairs, u_tab, s_tab, rhs, out,
    work_a, work_b, part, got, half, got_x, own, got_y, got_z,
    c_s, c_r, x_s, x_r, y_s, y_r, z_s, z_r,
):
    x, y, zh, zl, core = here()
    z = zh * 2 + zl

    def steps(k):
        far = k < FAR
        r = lax.rem(k, 3)
        dx = jnp.where(far, 1 + 2 * r - 3 * lax.div(r, 2), 0)
        return dx, lax.rem(jnp.where(far, lax.div(k, 3), k - FAR) + 1, 4)

    def gather(n, work, low, high):
        k, wh = lax.div(n, 2), lax.rem(n, 2)
        dx, dy = steps(k)
        tx, ty = lax.rem(x + dx, 4), lax.rem(y + dy, 4)
        base = (wh * 16 + tx * 4 + lax.div(ty, 2)) * 256 + lax.rem(ty, 2) * 64
        numbers = pairs.at[pl.ds(pl.multiple_of(base, 8), 704)]
        for e in range(low, high):
            at = (e // 64) * 512 + e % 64
            i, j = numbers[at], numbers[at + 128]
            for h in range(2):
                total = None
                for d in range(3):
                    row = h * 24 + d * 8
                    term = u_tab[i, row : row + 8, :] * s_tab[j, row : row + 8, :]
                    total = term if total is None else total + term
                work[(h * BLOCK + e) * 9 : (h * BLOCK + e) * 9 + 8, :] = total

    def project(n, now, later):
        nxt = jnp.minimum(n + 1, 2 * PIECES - 1)
        value = None
        for t in range(6):
            h, r = t // 3, t % 3 * 2
            parts = [split(now[pl.ds(h * BLOCK * 9 + r + k, BLOCK, stride=9), :]) for k in range(2)]
            high, low = (jnp.concatenate([p[k] for p in parts], axis=1) for k in range(2))
            wide = dot(high, rhs[t * 256 : t * 256 + 256, :])
            narrow = dot(low, rhs[t * 256 : t * 256 + 256, 0:128])
            term = wide[:, 0:128] + (wide[:, 128:256] + narrow)
            value = term if value is None else value + term
            gather(nxt, later, CUTS[t], CUTS[t + 1])
        value = value * factor
        k, wh = lax.div(n, 2), lax.rem(n, 2)
        for u in range(2):
            for c in range(2):
                part[k, c, wh * 2 + u] = value[(2 * u + c) * 32 : (2 * u + c) * 32 + 32, :]

    def c_copy(k):
        return pltpu.make_async_remote_copy(
            src_ref=part.at[k, 1 - core], dst_ref=got.at[k], send_sem=c_s.at[k], recv_sem=c_r.at[k],
            device_id=device(flip=1), device_id_type=MESH,
        )

    def x_copy(k):
        return pltpu.make_async_remote_copy(
            src_ref=half.at[k], dst_ref=got_x.at[k], send_sem=x_s.at[k], recv_sem=x_r.at[k],
            device_id=device(dx=steps(k)[0]), device_id_type=MESH,
        )

    def y_copy(o):
        return pltpu.make_async_remote_copy(
            src_ref=own.at[o], dst_ref=got_y.at[o], send_sem=y_s.at[o], recv_sem=y_r.at[o],
            device_id=device(dy=o + 1), device_id_type=MESH,
        )

    def z_copy(o):
        return pltpu.make_async_remote_copy(
            src_ref=own.at[3, lax.rem(z + o + 1, 4)], dst_ref=got_z.at[o],
            send_sem=z_s.at[o], recv_sem=z_r.at[o], device_id=device(dz=o + 1), device_id_type=MESH,
        )

    def far_piece(k):
        c_copy(k).wait_recv()
        half[k] = part[k, core] + got[k]
        x_copy(k).start()

    def near_piece(o):
        c_copy(FAR + o).wait_recv()
        for r in range(3):
            x_copy(3 * o + r).wait_recv()
        own[o] = (part[FAR + o, core] + got[FAR + o]) + (got_x[3 * o] + (got_x[3 * o + 1] + got_x[3 * o + 2]))
        if o < 3:
            y_copy(o).start()

    def trip(m, _):
        for parity, (now, later) in enumerate(((work_a, work_b), (work_b, work_a))):
            @pl.when(lax.rem(m, 2) == parity)
            def _():
                project(m, now, later)

        k = lax.div(m, 2)

        @pl.when(lax.rem(m, 2) == 1)
        def _():
            c_copy(k).start()

        @pl.when((lax.rem(m, 2) == 1) & (k > 1) & (k < FAR + 2))
        def _():
            far_piece(k - 2)

        for o in range(2):
            @pl.when(m == 2 * FAR + 4 + 2 * o)
            def _():
                near_piece(o)

        return 0

    gather(0, work_a, 0, BLOCK)
    lax.fori_loop(0, 2 * PIECES, trip, 0)
    near_piece(2)
    near_piece(3)
    for o in range(3):
        y_copy(o).wait_recv()
    own[3] = own[3] + (got_y[0] + (got_y[1] + got_y[2]))
    for o in (0, 2, 1):
        z_copy(o).start()
    for o in range(3):
        z_copy(o).wait_recv()
    out[...] = own[3, z] + (got_z[0] + (got_z[1] + got_z[2]))
    for k in range(PIECES):
        c_copy(k).wait_send()
    for k in range(FAR):
        x_copy(k).wait_send()
    for o in range(3):
        y_copy(o).wait_send()
        z_copy(o).wait_send()


def whole_kernel(factor, pairs_hbm, snaps_hbm, coeffs_hbm, out, *scratch):
    pairs, pairs_sem, u_tab, s_tab, rhs, *rest = scratch
    first, second = rest[:17], rest[17:]
    load = pltpu.make_async_copy(pairs_hbm, pairs, pairs_sem)
    load.start()
    others = [device(flip=1)]
    for k in range(1, 4):
        others += [device(dx=k), device(dy=k), device(dz=k)]
    tables_kernel(others, snaps_hbm, coeffs_hbm, u_tab, s_tab, rhs, *first)
    load.wait()
    u_tab, s_tab = (tab.reshape(MODES, STEP, LANES) for tab in (u_tab, s_tab))
    pairs_kernel(factor, pairs, u_tab, s_tab, rhs, out, *second)


def shards(snapshots, coeffs, pair_table):
    dma = pltpu.SemaphoreType.DMA
    piece = (4, 32, MODES)
    hbm = pl.BlockSpec(memory_space=pltpu.HBM)
    return pl.pallas_call(
        functools.partial(whole_kernel, 0.5 / 256.0),
        out_shape=jax.ShapeDtypeStruct((32, MODES), F32),
        in_specs=[hbm, hbm, hbm],
        out_specs=pl.BlockSpec(memory_space=pltpu.VMEM),
        scratch_shapes=[
            pltpu.SMEM((2 * PAIRS,), jnp.int32),
            dma,
            pltpu.VMEM((MODES * STEP, LANES), F32),
            pltpu.VMEM((MODES * STEP, LANES), F32),
            pltpu.VMEM((12 * LANES, 256), BF16),
            pltpu.VMEM((32 * 96, LANES), F32),
            pltpu.VMEM((256, MODES), F32),
            pltpu.VMEM((8, 12, 32, LANES), F32),
            pltpu.VMEM((12, 256, LANES), F32),
            pltpu.VMEM((12, MODES, LANES), F32),
            pltpu.VMEM((12, MODES, LANES), F32),
            pltpu.VMEM((12, MODES, LANES), F32),
            pltpu.VMEM((3, MODES, LANES), F32),
            pltpu.VMEM((3, MODES, LANES), F32),
            dma((2,)), dma, dma((3, 8)), dma((3, 8)), dma((3, 2)), dma((3, 2)), dma((3, 2)), dma((3, 2)),
            pltpu.VMEM((2 * BLOCK * 9 + 8, LANES), F32),
            pltpu.VMEM((2 * BLOCK * 9 + 8, LANES), F32),
            pltpu.VMEM((PIECES, 2, *piece), F32),
            pltpu.VMEM((PIECES, *piece), F32),
            pltpu.VMEM((FAR, *piece), F32),
            pltpu.VMEM((FAR, *piece), F32),
            pltpu.VMEM((4, *piece), F32),
            pltpu.VMEM((3, *piece), F32),
            pltpu.VMEM((3, 32, MODES), F32),
            dma((PIECES,)), dma((PIECES,)), dma((FAR,)), dma((FAR,)),
            dma((3,)), dma((3,)), dma((3,)), dma((3,)),
        ],
        compiler_params=pltpu.CompilerParams(
            collective_id=0, has_side_effects=True, vmem_limit_bytes=60 * 2**20
        ),
        name="whole",
    )(
        pair_table.reshape(32, 128, 2).transpose(0, 2, 1).reshape(-1),
        snapshots.reshape(32 * 96, LANES),
        coeffs,
    )


def solution(mesh):
    placed = (P("tm", None, "space", None, None), P(), P())
    return jax.shard_map(
        shards, mesh=mesh, in_specs=placed, out_specs=P(("tm", "space"), None), check_vma=False
    )
```

```python
import functools

import jax
import jax.numpy as jnp
from jax import lax
from jax.experimental import pallas as pl
from jax.experimental.pallas import tpu as pltpu
from jax.sharding import PartitionSpec as P

MESH = pl.DeviceIdType.MESH
F32 = jnp.float32
BF16 = jnp.bfloat16
MODES = 128
LANES = 128
PAIRS = 4096
STEP = 56
BLOCK = 128


def here():
    t, s = lax.axis_index("tm"), lax.axis_index("space")
    return lax.rem(t, 4), lax.rem(lax.div(s, 2), 4), lax.div(t, 4), lax.div(s, 8), lax.rem(s, 2)


def there(x, y, zh, zl, core):
    return zh * 4 + x, zl * 8 + y * 2 + core


def band_of(x, zh):
    return x + zh * (7 - 2 * x)


def owner_of(band):
    zh = lax.div(band, 4)
    return zh * 4 + band + zh * (7 - 2 * band)


def split(value):
    high = value.astype(BF16)
    return high, (value - high.astype(F32)).astype(BF16)


def dot(a, b):
    return jnp.dot(a, b, preferred_element_type=F32)


ORDER = (5, 2, 7, 4, 1, 6, 3)
SPANS = ((0, 5), (5, 9), (9, 12))


def tables_kernel(
    others, snaps_hbm, coeffs_hbm, u_tab, s_tab, rhs, snaps, coeffs, send, recv, modes, below, above, low, high,
    in_sem, own_sem, a2a_s, a2a_r, x_s, x_r, y_s, y_r,
):
    x, y, zh, zl, core = here()
    tm, space = lax.axis_index("tm"), lax.axis_index("space")
    band = band_of(x, zh)
    after, before = lax.rem(space + 1, 16), lax.rem(space + 15, 16)
    loads = [
        pltpu.make_async_copy(snaps_hbm, snaps, in_sem.at[0]),
        pltpu.make_async_copy(coeffs_hbm, coeffs, in_sem.at[1]),
    ]
    for load in loads:
        load.start()

    def partner(rel):
        return lax.rem(zh + rel // 4, 2) * 4 + lax.rem(x + rel % 4, 4)

    barrier = pltpu.get_barrier_semaphore()
    for rel in range(1, 8):
        pl.semaphore_signal(barrier, inc=1, device_id=(partner(rel), space), device_id_type=MESH)
    for side in (after, before):
        pl.semaphore_signal(barrier, inc=1, device_id=(tm, side), device_id_type=MESH)
    for target in others:
        pl.semaphore_signal(barrier, inc=1, device_id=target, device_id_type=MESH)

    loads[0].wait()
    for b in range(8):
        for c in range(3):
            for r in range(4):
                send[b, c * 4 + r] = snaps[pl.ds(c * 32 + 4 * b + r, 32, stride=96), :]
    own = pltpu.make_async_copy(send.at[band], recv.at[:, pl.ds(tm * 32, 32), :], own_sem)
    own.start()
    pl.semaphore_wait(barrier, 9 + len(others))

    def exchange(g, rel):
        first, last = SPANS[g]
        t = partner(rel)
        zt, xt = lax.div(t, 4), lax.rem(t, 4)
        return pltpu.make_async_remote_copy(
            src_ref=send.at[band_of(xt, zt), pl.ds(first, last - first)],
            dst_ref=recv.at[pl.ds(first, last - first), pl.ds(tm * 32, 32), :],
            send_sem=a2a_s.at[g, rel], recv_sem=a2a_r.at[g, rel],
            device_id=(t, space), device_id_type=MESH,
        )

    def x_copy(g, up):
        first, last = SPANS[g]
        return pltpu.make_async_remote_copy(
            src_ref=modes.at[pl.ds(first, last - first)],
            dst_ref=(below if up else above).at[pl.ds(first, last - first)],
            send_sem=x_s.at[g, up], recv_sem=x_r.at[g, up],
            device_id=(tm, after if up else before), device_id_type=MESH,
        )

    def y_copy(c, up):
        target = owner_of(jnp.minimum(band + 1, 7) if up else jnp.maximum(band - 1, 0))
        return pltpu.make_async_remote_copy(
            src_ref=modes.at[c * 4 + (3 if up else 0)],
            dst_ref=(low if up else high).at[c],
            send_sem=y_s.at[c, up], recv_sem=y_r.at[c, up],
            device_id=(target, space), device_id_type=MESH,
        )

    for g in range(len(SPANS)):
        for rel in ORDER:
            exchange(g, rel).start()

    @pl.when(band == 0)
    def _():
        low[...] = jnp.zeros_like(low)

    @pl.when(band == 7)
    def _():
        high[...] = jnp.zeros_like(high)

    loads[1].wait()
    coeff_high, coeff_low = split(coeffs[...].T)
    own.wait()

    def place(row):
        c, r = row // 4, row % 4
        return c, r, r // 2 * 24 + r % 2

    for g, (first, last) in enumerate(SPANS):
        for rel in ORDER:
            exchange(g, rel).wait_recv()
        rows = jnp.concatenate([recv[row] for row in range(first, last)], axis=1)
        row_high, row_low = split(rows)
        field = dot(coeff_high, row_high) + dot(coeff_high, row_low) + dot(coeff_low, row_high)
        for row in range(first, last):
            modes[row] = field[:, (row - first) * 128 : (row - first) * 128 + 128]
        for up in (1, 0):
            x_copy(g, up).start()
        for row in range(first, last):
            c, r, _ = place(row)
            if r == 3:
                @pl.when(band < 7)
                def _():
                    y_copy(c, 1).start()
            if r == 0:
                @pl.when(band > 0)
                def _():
                    y_copy(c, 0).start()

    for row in range(12):
        c, r, slot = place(row)
        value = modes[row]
        for copy in range(3):
            u_tab[pl.ds(slot + c * 8 + 2 * copy, MODES, stride=STEP), :] = value
        turned_high, turned_low = split(value.T)
        at = (r // 2 * 6 + c * 2 + r % 2) * LANES
        rhs[at : at + LANES, 0:128] = turned_high
        rhs[at : at + LANES, 128:256] = turned_low
        slope = pltpu.roll(value, 127, 1) - pltpu.roll(value, 1, 1)
        s_tab[pl.ds(slot + 16 + c * 2, MODES, stride=STEP), :] = slope

    for row in range(12):
        c, r, slot = place(row)
        if r in (1, 2):
            s_tab[pl.ds(slot + 8 + c * 2, MODES, stride=STEP), :] = modes[row + 1] - modes[row - 1]
    for g, (first, last) in enumerate(SPANS):
        for row in range(first, last):
            c, r, slot = place(row)
            if r == 0:
                @pl.when(band > 0)
                def _():
                    y_copy(c, 1).wait_recv()
                s_tab[pl.ds(slot + 8 + c * 2, MODES, stride=STEP), :] = modes[row + 1] - low[c]
            if r == 3:
                @pl.when(band < 7)
                def _():
                    y_copy(c, 0).wait_recv()
                s_tab[pl.ds(slot + 8 + c * 2, MODES, stride=STEP), :] = high[c] - modes[row - 1]
        for up in (1, 0):
            x_copy(g, up).wait_recv()
        for row in range(first, last):
            c, r, slot = place(row)
            s_tab[pl.ds(slot + c * 2, MODES, stride=STEP), :] = above[row] - below[row]

    for c in range(3):
        for rel in ORDER:
            exchange(c, rel).wait_send()
        for up in (1, 0):
            x_copy(c, up).wait_send()

        @pl.when(band < 7)
        def _():
            y_copy(c, 1).wait_send()

        @pl.when(band > 0)
        def _():
            y_copy(c, 0).wait_send()


def device(dx=0, dy=0, dz=0, flip=0):
    x, y, zh, zl, core = here()
    tz = lax.rem(zh * 2 + zl + dz, 4)
    tx, ty = lax.rem(x + dx, 4), lax.rem(y + dy, 4)
    return there(tx, ty, lax.div(tz, 2), lax.rem(tz, 2), 1 - core if flip else core)


PIECES = 16
FAR = 12
CUTS = (0, 16, 36, 56, 76, 96, 128)


def pairs_kernel(
    factor, pairs, u_tab, s_tab, rhs, out,
    work_a, work_b, part, got, half, got_x, own, got_f,
    c_s, c_r, x_s, x_r, f_s, f_r,
):
    x, y, zh, zl, core = here()
    z = zh * 2 + zl

    def steps(k):
        far = k < FAR
        r = lax.rem(k, 3)
        dx = jnp.where(far, 1 + 2 * r - 3 * lax.div(r, 2), 0)
        return dx, lax.rem(jnp.where(far, lax.div(k, 3), k - FAR) + 1, 4)

    def gather(n, work, low, high):
        k, wh = lax.div(n, 2), lax.rem(n, 2)
        dx, dy = steps(k)
        tx, ty = lax.rem(x + dx, 4), lax.rem(y + dy, 4)
        base = (wh * 16 + tx * 4 + lax.div(ty, 2)) * 256 + lax.rem(ty, 2) * 64
        numbers = pairs.at[pl.ds(pl.multiple_of(base, 8), 704)]
        for e in range(low, high):
            at = (e // 64) * 512 + e % 64
            i, j = numbers[at], numbers[at + 128]
            for h in range(2):
                total = None
                for d in range(3):
                    row = h * 24 + d * 8
                    term = u_tab[i, row : row + 8, :] * s_tab[j, row : row + 8, :]
                    total = term if total is None else total + term
                work[(h * BLOCK + e) * 9 : (h * BLOCK + e) * 9 + 8, :] = total

    def project(n, now, later):
        nxt = jnp.minimum(n + 1, 2 * PIECES - 1)
        value = None
        for t in range(6):
            h, r = t // 3, t % 3 * 2
            parts = [split(now[pl.ds(h * BLOCK * 9 + r + k, BLOCK, stride=9), :]) for k in range(2)]
            high, low = (jnp.concatenate([p[k] for p in parts], axis=1) for k in range(2))
            wide = dot(high, rhs[t * 256 : t * 256 + 256, :])
            narrow = dot(low, rhs[t * 256 : t * 256 + 256, 0:128])
            term = wide[:, 0:128] + (wide[:, 128:256] + narrow)
            value = term if value is None else value + term
            gather(nxt, later, CUTS[t], CUTS[t + 1])
        value = value * factor
        k, wh = lax.div(n, 2), lax.rem(n, 2)
        for u in range(2):
            for c in range(2):
                part[k, c, wh * 2 + u] = value[(2 * u + c) * 32 : (2 * u + c) * 32 + 32, :]

    def c_copy(k):
        return pltpu.make_async_remote_copy(
            src_ref=part.at[k, 1 - core], dst_ref=got.at[k], send_sem=c_s.at[k], recv_sem=c_r.at[k],
            device_id=device(flip=1), device_id_type=MESH,
        )

    def x_copy(k):
        return pltpu.make_async_remote_copy(
            src_ref=half.at[k], dst_ref=got_x.at[k], send_sem=x_s.at[k], recv_sem=x_r.at[k],
            device_id=device(dx=steps(k)[0]), device_id_type=MESH,
        )

    def f_copy(o, dz):
        return pltpu.make_async_remote_copy(
            src_ref=own.at[o, lax.rem(z + dz, 4)], dst_ref=got_f.at[o, dz],
            send_sem=f_s.at[o, dz], recv_sem=f_r.at[o, dz],
            device_id=device(dy=(o + 1) % 4, dz=dz), device_id_type=MESH,
        )

    def far_piece(k):
        c_copy(k).wait_recv()
        half[k] = part[k, core] + got[k]
        x_copy(k).start()

    def near_piece(o):
        c_copy(FAR + o).wait_recv()
        for r in range(3):
            x_copy(3 * o + r).wait_recv()
        own[o] = (part[FAR + o, core] + got[FAR + o]) + (got_x[3 * o] + (got_x[3 * o + 1] + got_x[3 * o + 2]))
        for dz in (2, 1, 3, 0):
            if o < 3 or dz:
                f_copy(o, dz).start()

    def trip(m, _):
        for parity, (now, later) in enumerate(((work_a, work_b), (work_b, work_a))):
            @pl.when(lax.rem(m, 2) == parity)
            def _():
                project(m, now, later)

        k = lax.div(m, 2)

        @pl.when(lax.rem(m, 2) == 1)
        def _():
            c_copy(k).start()

        @pl.when((lax.rem(m, 2) == 1) & (k > 1) & (k < FAR + 2))
        def _():
            far_piece(k - 2)

        for o in range(2):
            @pl.when(m == 2 * FAR + 4 + 2 * o)
            def _():
                near_piece(o)

        return 0

    gather(0, work_a, 0, BLOCK)
    lax.fori_loop(0, 2 * PIECES, trip, 0)
    near_piece(2)
    near_piece(3)
    total = own[3, z]
    for o in range(4):
        for dz in range(4):
            if o < 3 or dz:
                f_copy(o, dz).wait_recv()
                total = total + got_f[o, dz]
    out[...] = total
    for k in range(PIECES):
        c_copy(k).wait_send()
    for k in range(FAR):
        x_copy(k).wait_send()
    for o in range(4):
        for dz in range(4):
            if o < 3 or dz:
                f_copy(o, dz).wait_send()


def whole_kernel(factor, pairs_hbm, snaps_hbm, coeffs_hbm, out, *scratch):
    pairs, pairs_sem, u_tab, s_tab, rhs, *rest = scratch
    first, second = rest[:17], rest[17:]
    load = pltpu.make_async_copy(pairs_hbm, pairs, pairs_sem)
    load.start()
    others = [device(flip=1)]
    others += [device(dx=k) for k in range(1, 4)]
    others += [device(dy=k // 4, dz=k % 4) for k in range(1, 16)]
    tables_kernel(others, snaps_hbm, coeffs_hbm, u_tab, s_tab, rhs, *first)
    load.wait()
    u_tab, s_tab = (tab.reshape(MODES, STEP, LANES) for tab in (u_tab, s_tab))
    pairs_kernel(factor, pairs, u_tab, s_tab, rhs, out, *second)


def shards(snapshots, coeffs, pair_table):
    dma = pltpu.SemaphoreType.DMA
    piece = (4, 32, MODES)
    hbm = pl.BlockSpec(memory_space=pltpu.HBM)
    return pl.pallas_call(
        functools.partial(whole_kernel, 0.5 / 256.0),
        out_shape=jax.ShapeDtypeStruct((32, MODES), F32),
        in_specs=[hbm, hbm, hbm],
        out_specs=pl.BlockSpec(memory_space=pltpu.VMEM),
        scratch_shapes=[
            pltpu.SMEM((2 * PAIRS,), jnp.int32),
            dma,
            pltpu.VMEM((MODES * STEP, LANES), F32),
            pltpu.VMEM((MODES * STEP, LANES), F32),
            pltpu.VMEM((12 * LANES, 256), BF16),
            pltpu.VMEM((32 * 96, LANES), F32),
            pltpu.VMEM((256, MODES), F32),
            pltpu.VMEM((8, 12, 32, LANES), F32),
            pltpu.VMEM((12, 256, LANES), F32),
            pltpu.VMEM((12, MODES, LANES), F32),
            pltpu.VMEM((12, MODES, LANES), F32),
            pltpu.VMEM((12, MODES, LANES), F32),
            pltpu.VMEM((3, MODES, LANES), F32),
            pltpu.VMEM((3, MODES, LANES), F32),
            dma((2,)), dma, dma((3, 8)), dma((3, 8)), dma((3, 2)), dma((3, 2)), dma((3, 2)), dma((3, 2)),
            pltpu.VMEM((2 * BLOCK * 9 + 8, LANES), F32),
            pltpu.VMEM((2 * BLOCK * 9 + 8, LANES), F32),
            pltpu.VMEM((PIECES, 2, *piece), F32),
            pltpu.VMEM((PIECES, *piece), F32),
            pltpu.VMEM((FAR, *piece), F32),
            pltpu.VMEM((FAR, *piece), F32),
            pltpu.VMEM((4, *piece), F32),
            pltpu.VMEM((4, *piece), F32),
            dma((PIECES,)), dma((PIECES,)), dma((FAR,)), dma((FAR,)), dma((4, 4)), dma((4, 4)),
        ],
        compiler_params=pltpu.CompilerParams(
            collective_id=0, has_side_effects=True, vmem_limit_bytes=60 * 2**20
        ),
        name="whole",
    )(
        pair_table.reshape(32, 128, 2).transpose(0, 2, 1).reshape(-1),
        snapshots.reshape(32 * 96, LANES),
        coeffs,
    )


def solution(mesh):
    placed = (P("tm", None, "space", None, None), P(), P())
    return jax.shard_map(
        shards, mesh=mesh, in_specs=placed, out_specs=P(("tm", "space"), None), check_vma=False
    )
```

```python
import functools

import jax
import jax.numpy as jnp
from jax import lax
from jax.experimental import pallas as pl
from jax.experimental.pallas import tpu as pltpu
from jax.sharding import PartitionSpec as P

MESH = pl.DeviceIdType.MESH
F32 = jnp.float32
BF16 = jnp.bfloat16
MODES = 128
LANES = 128
PAIRS = 4096
STEP = 56
BLOCK = 128


def here():
    t, s = lax.axis_index("tm"), lax.axis_index("space")
    return lax.rem(t, 4), lax.rem(lax.div(s, 2), 4), lax.div(t, 4), lax.div(s, 8), lax.rem(s, 2)


def there(x, y, zh, zl, core):
    return zh * 4 + x, zl * 8 + y * 2 + core


def band_of(x, zh):
    return x + zh * (7 - 2 * x)


def owner_of(band):
    zh = lax.div(band, 4)
    return zh * 4 + band + zh * (7 - 2 * band)


def split(value):
    high = value.astype(BF16)
    return high, (value - high.astype(F32)).astype(BF16)


def dot(a, b):
    return jnp.dot(a, b, preferred_element_type=F32)


ORDER = (5, 2, 7, 4, 1, 6, 3)
SPANS = ((0, 5), (5, 9), (9, 12))


def tables_kernel(
    others, snaps_hbm, coeffs_hbm, u_tab, s_tab, rhs, snaps, coeffs, send, recv, modes, below, above, low, high,
    in_sem, own_sem, a2a_s, a2a_r, x_s, x_r, y_s, y_r,
):
    x, y, zh, zl, core = here()
    tm, space = lax.axis_index("tm"), lax.axis_index("space")
    band = band_of(x, zh)
    after, before = lax.rem(space + 1, 16), lax.rem(space + 15, 16)
    loads = [
        pltpu.make_async_copy(snaps_hbm, snaps, in_sem.at[0]),
        pltpu.make_async_copy(coeffs_hbm, coeffs, in_sem.at[1]),
    ]
    for load in loads:
        load.start()

    def partner(rel):
        return lax.rem(zh + rel // 4, 2) * 4 + lax.rem(x + rel % 4, 4)

    barrier = pltpu.get_barrier_semaphore()
    for rel in range(1, 8):
        pl.semaphore_signal(barrier, inc=1, device_id=(partner(rel), space), device_id_type=MESH)
    for side in (after, before):
        pl.semaphore_signal(barrier, inc=1, device_id=(tm, side), device_id_type=MESH)
    for target in others:
        pl.semaphore_signal(barrier, inc=1, device_id=target, device_id_type=MESH)

    loads[0].wait()
    def exchange(g, rel):
        first, last = SPANS[g]
        t = partner(rel)
        zt, xt = lax.div(t, 4), lax.rem(t, 4)
        return pltpu.make_async_remote_copy(
            src_ref=send.at[band_of(xt, zt), pl.ds(first, last - first)],
            dst_ref=recv.at[pl.ds(first, last - first), pl.ds(tm * 32, 32), :],
            send_sem=a2a_s.at[g, rel], recv_sem=a2a_r.at[g, rel],
            device_id=(t, space), device_id_type=MESH,
        )

    def x_copy(g, up):
        first, last = SPANS[g]
        return pltpu.make_async_remote_copy(
            src_ref=modes.at[pl.ds(first, last - first)],
            dst_ref=(below if up else above).at[pl.ds(first, last - first)],
            send_sem=x_s.at[g, up], recv_sem=x_r.at[g, up],
            device_id=(tm, after if up else before), device_id_type=MESH,
        )

    def y_copy(c, up):
        target = owner_of(jnp.minimum(band + 1, 7) if up else jnp.maximum(band - 1, 0))
        return pltpu.make_async_remote_copy(
            src_ref=modes.at[c * 4 + (3 if up else 0)],
            dst_ref=(low if up else high).at[c],
            send_sem=y_s.at[c, up], recv_sem=y_r.at[c, up],
            device_id=(target, space), device_id_type=MESH,
        )

    for g, (first, last) in enumerate(SPANS):
        for row in range(first, last):
            for b in range(8):
                send[b, row] = snaps[pl.ds(row // 4 * 32 + 4 * b + row % 4, 32, stride=96), :]
        if g == 0:
            pl.semaphore_wait(barrier, 9 + len(others))
        for rel in ORDER:
            exchange(g, rel).start()
    own = pltpu.make_async_copy(send.at[band], recv.at[:, pl.ds(tm * 32, 32), :], own_sem)
    own.start()

    @pl.when(band == 0)
    def _():
        low[...] = jnp.zeros_like(low)

    @pl.when(band == 7)
    def _():
        high[...] = jnp.zeros_like(high)

    loads[1].wait()
    coeff_high, coeff_low = split(coeffs[...].T)
    own.wait()

    def place(row):
        c, r = row // 4, row % 4
        return c, r, r // 2 * 24 + r % 2

    for g, (first, last) in enumerate(SPANS):
        for rel in ORDER:
            exchange(g, rel).wait_recv()
        rows = jnp.concatenate([recv[row] for row in range(first, last)], axis=1)
        row_high, row_low = split(rows)
        field = dot(coeff_high, row_high) + dot(coeff_high, row_low) + dot(coeff_low, row_high)
        for row in range(first, last):
            modes[row] = field[:, (row - first) * 128 : (row - first) * 128 + 128]
        for up, crossing in ((1, y * 2 + core == 7), (0, y * 2 + core == 0)):
            @pl.when(jnp.logical_not(crossing))
            def _():
                x_copy(g, up).start()

            if g > 0:
                @pl.when(crossing)
                def _():
                    for late in range(g * 2 - 2, g + 1):
                        x_copy(late, up).start()
        for row in range(first, last):
            c, r, _ = place(row)
            if r == 3:
                @pl.when(band < 7)
                def _():
                    y_copy(c, 1).start()
            if r == 0:
                @pl.when(band > 0)
                def _():
                    y_copy(c, 0).start()

    for row in range(12):
        c, r, slot = place(row)
        value = modes[row]
        for copy in range(3):
            u_tab[pl.ds(slot + c * 8 + 2 * copy, MODES, stride=STEP), :] = value
        turned_high, turned_low = split(value.T)
        at = (r // 2 * 6 + c * 2 + r % 2) * LANES
        rhs[at : at + LANES, 0:128] = turned_high
        rhs[at : at + LANES, 128:256] = turned_low
        slope = pltpu.roll(value, 127, 1) - pltpu.roll(value, 1, 1)
        s_tab[pl.ds(slot + 16 + c * 2, MODES, stride=STEP), :] = slope

    for row in range(12):
        c, r, slot = place(row)
        if r in (1, 2):
            s_tab[pl.ds(slot + 8 + c * 2, MODES, stride=STEP), :] = modes[row + 1] - modes[row - 1]
    for g, (first, last) in enumerate(SPANS):
        for row in range(first, last):
            c, r, slot = place(row)
            if r == 0:
                @pl.when(band > 0)
                def _():
                    y_copy(c, 1).wait_recv()
                s_tab[pl.ds(slot + 8 + c * 2, MODES, stride=STEP), :] = modes[row + 1] - low[c]
            if r == 3:
                @pl.when(band < 7)
                def _():
                    y_copy(c, 0).wait_recv()
                s_tab[pl.ds(slot + 8 + c * 2, MODES, stride=STEP), :] = high[c] - modes[row - 1]
        for up in (1, 0):
            x_copy(g, up).wait_recv()
        for row in range(first, last):
            c, r, slot = place(row)
            s_tab[pl.ds(slot + c * 2, MODES, stride=STEP), :] = above[row] - below[row]

    for c in range(3):
        for rel in ORDER:
            exchange(c, rel).wait_send()
        for up in (1, 0):
            x_copy(c, up).wait_send()

        @pl.when(band < 7)
        def _():
            y_copy(c, 1).wait_send()

        @pl.when(band > 0)
        def _():
            y_copy(c, 0).wait_send()


def device(dx=0, dy=0, dz=0, flip=0):
    x, y, zh, zl, core = here()
    tz = lax.rem(zh * 2 + zl + dz, 4)
    tx, ty = lax.rem(x + dx, 4), lax.rem(y + dy, 4)
    return there(tx, ty, lax.div(tz, 2), lax.rem(tz, 2), 1 - core if flip else core)


PIECES = 16
FAR = 12
CUTS = (0, 12, 28, 46, 66, 92, 128)


def pairs_kernel(
    factor, pairs, u_tab, s_tab, rhs, out,
    work_a, work_b, part, got, half, got_x, own, got_f,
    c_s, c_r, x_s, x_r, f_s, f_r,
):
    x, y, zh, zl, core = here()
    z = zh * 2 + zl

    def steps(k):
        far = k < FAR
        r = lax.rem(k, 3)
        dx = jnp.where(far, 1 + 2 * r - 3 * lax.div(r, 2), 0)
        return dx, lax.rem(jnp.where(far, lax.div(k, 3), k - FAR) + 1, 4)

    def gather(n, work, low, high):
        k, wh = lax.div(n, 2), lax.rem(n, 2)
        dx, dy = steps(k)
        tx, ty = lax.rem(x + dx, 4), lax.rem(y + dy, 4)
        base = (wh * 16 + tx * 4 + lax.div(ty, 2)) * 256 + lax.rem(ty, 2) * 64
        numbers = pairs.at[pl.ds(pl.multiple_of(base, 8), 704)]
        for e in range(low, high):
            at = (e // 64) * 512 + e % 64
            i, j = numbers[at], numbers[at + 128]
            for h in range(2):
                total = None
                for d in range(3):
                    row = h * 24 + d * 8
                    term = u_tab[i, row : row + 8, :] * s_tab[j, row : row + 8, :]
                    total = term if total is None else total + term
                work[(h * BLOCK + e) * 9 : (h * BLOCK + e) * 9 + 8, :] = total

    def project(n, now, later):
        nxt = jnp.minimum(n + 1, 2 * PIECES - 1)
        value = None
        for t in range(6):
            h, r = t // 3, t % 3 * 2
            parts = [split(now[pl.ds(h * BLOCK * 9 + r + k, BLOCK, stride=9), :]) for k in range(2)]
            high, low = (jnp.concatenate([p[k] for p in parts], axis=1) for k in range(2))
            wide = dot(high, rhs[t * 256 : t * 256 + 256, :])
            narrow = dot(low, rhs[t * 256 : t * 256 + 256, 0:128])
            term = wide[:, 0:128] + (wide[:, 128:256] + narrow)
            value = term if value is None else value + term
            gather(nxt, later, CUTS[t], CUTS[t + 1])
        value = value * factor
        k, wh = lax.div(n, 2), lax.rem(n, 2)
        for u in range(2):
            for c in range(2):
                part[k, c, wh * 2 + u] = value[(2 * u + c) * 32 : (2 * u + c) * 32 + 32, :]

    def c_copy(k):
        return pltpu.make_async_remote_copy(
            src_ref=part.at[k, 1 - core], dst_ref=got.at[k], send_sem=c_s.at[k], recv_sem=c_r.at[k],
            device_id=device(flip=1), device_id_type=MESH,
        )

    def x_copy(k):
        return pltpu.make_async_remote_copy(
            src_ref=half.at[k], dst_ref=got_x.at[k], send_sem=x_s.at[k], recv_sem=x_r.at[k],
            device_id=device(dx=steps(k)[0]), device_id_type=MESH,
        )

    def f_copy(o, dz):
        return pltpu.make_async_remote_copy(
            src_ref=own.at[o, lax.rem(z + dz, 4)], dst_ref=got_f.at[o, dz],
            send_sem=f_s.at[o, dz], recv_sem=f_r.at[o, dz],
            device_id=device(dy=(o + 1) % 4, dz=dz), device_id_type=MESH,
        )

    def far_piece(k):
        c_copy(k).wait_recv()
        half[k] = part[k, core] + got[k]
        x_copy(k).start()

    def near_piece(o):
        c_copy(FAR + o).wait_recv()
        for r in range(3):
            x_copy(3 * o + r).wait_recv()
        own[o] = (part[FAR + o, core] + got[FAR + o]) + (got_x[3 * o] + (got_x[3 * o + 1] + got_x[3 * o + 2]))
        for dz in (2, 1, 3, 0):
            if o < 3 or dz:
                f_copy(o, dz).start()

    def trip(m, _):
        for parity, (now, later) in enumerate(((work_a, work_b), (work_b, work_a))):
            @pl.when(lax.rem(m, 2) == parity)
            def _():
                project(m, now, later)

        k = lax.div(m, 2)

        @pl.when(lax.rem(m, 2) == 1)
        def _():
            c_copy(k).start()

        @pl.when((lax.rem(m, 2) == 1) & (k > 1) & (k < FAR + 2))
        def _():
            far_piece(k - 2)

        for o in range(2):
            @pl.when(m == 2 * FAR + 4 + 2 * o)
            def _():
                near_piece(o)

        return 0

    gather(0, work_a, 0, BLOCK)
    lax.fori_loop(0, 2 * PIECES, trip, 0)
    near_piece(2)
    near_piece(3)
    total = own[3, z]
    for o in range(4):
        for dz in range(4):
            if o < 3 or dz:
                f_copy(o, dz).wait_recv()
                total = total + got_f[o, dz]
    out[...] = total
    for k in range(PIECES):
        c_copy(k).wait_send()
    for k in range(FAR):
        x_copy(k).wait_send()
    for o in range(4):
        for dz in range(4):
            if o < 3 or dz:
                f_copy(o, dz).wait_send()


def whole_kernel(factor, pairs_hbm, snaps_hbm, coeffs_hbm, out, *scratch):
    pairs, pairs_sem, u_tab, s_tab, rhs, *rest = scratch
    first, second = rest[:17], rest[17:]
    load = pltpu.make_async_copy(pairs_hbm, pairs, pairs_sem)
    load.start()
    others = [device(flip=1)]
    others += [device(dx=k) for k in range(1, 4)]
    others += [device(dy=k // 4, dz=k % 4) for k in range(1, 16)]
    tables_kernel(others, snaps_hbm, coeffs_hbm, u_tab, s_tab, rhs, *first)
    load.wait()
    u_tab, s_tab = (tab.reshape(MODES, STEP, LANES) for tab in (u_tab, s_tab))
    pairs_kernel(factor, pairs, u_tab, s_tab, rhs, out, *second)


def shards(snapshots, coeffs, pair_table):
    dma = pltpu.SemaphoreType.DMA
    piece = (4, 32, MODES)
    hbm = pl.BlockSpec(memory_space=pltpu.HBM)
    return pl.pallas_call(
        functools.partial(whole_kernel, 0.5 / 256.0),
        out_shape=jax.ShapeDtypeStruct((32, MODES), F32),
        in_specs=[hbm, hbm, hbm],
        out_specs=pl.BlockSpec(memory_space=pltpu.VMEM),
        scratch_shapes=[
            pltpu.SMEM((2 * PAIRS,), jnp.int32),
            dma,
            pltpu.VMEM((MODES * STEP, LANES), F32),
            pltpu.VMEM((MODES * STEP, LANES), F32),
            pltpu.VMEM((12 * LANES, 256), BF16),
            pltpu.VMEM((32 * 96, LANES), F32),
            pltpu.VMEM((256, MODES), F32),
            pltpu.VMEM((8, 12, 32, LANES), F32),
            pltpu.VMEM((12, 256, LANES), F32),
            pltpu.VMEM((12, MODES, LANES), F32),
            pltpu.VMEM((12, MODES, LANES), F32),
            pltpu.VMEM((12, MODES, LANES), F32),
            pltpu.VMEM((3, MODES, LANES), F32),
            pltpu.VMEM((3, MODES, LANES), F32),
            dma((2,)), dma, dma((3, 8)), dma((3, 8)), dma((3, 2)), dma((3, 2)), dma((3, 2)), dma((3, 2)),
            pltpu.VMEM((2 * BLOCK * 9 + 8, LANES), F32),
            pltpu.VMEM((2 * BLOCK * 9 + 8, LANES), F32),
            pltpu.VMEM((PIECES, 2, *piece), F32),
            pltpu.VMEM((PIECES, *piece), F32),
            pltpu.VMEM((FAR, *piece), F32),
            pltpu.VMEM((FAR, *piece), F32),
            pltpu.VMEM((4, *piece), F32),
            pltpu.VMEM((4, *piece), F32),
            dma((PIECES,)), dma((PIECES,)), dma((FAR,)), dma((FAR,)), dma((4, 4)), dma((4, 4)),
        ],
        compiler_params=pltpu.CompilerParams(
            collective_id=0, has_side_effects=True, vmem_limit_bytes=60 * 2**20
        ),
        name="whole",
    )(
        pair_table.reshape(32, 128, 2).transpose(0, 2, 1).reshape(-1),
        snapshots.reshape(32 * 96, LANES),
        coeffs,
    )


def solution(mesh):
    placed = (P("tm", None, "space", None, None), P(), P())
    return jax.shard_map(
        shards, mesh=mesh, in_specs=placed, out_specs=P(("tm", "space"), None), check_vma=False
    )
```
